32 devices in a mesh: grp: 4 (over y, x), dev: 8 (over z, core).
Axes of the slice: x: 2, y: 2, z: 4, core: 2. Of those that a mesh axis runs over, the one named last changes fastest.
Arguments:
- ids: int32 [4096, 13, 2], P(('grp', 'dev')), may hold values from 0 to 65535, as said below
- location: int32 [65536], replicated, may hold values from 0 to 65535, as said below
- cold_table: bfloat16 [65536, 128], P(('grp', 'dev')), may hold values from -3 to 3
- hot_index: int32 [4096, 13], P(('grp', 'dev')), may hold values from 0 to 31
- hot_list: int32 [32, 32], P(('grp', 'dev')), may hold values from 0 to 4095, as said below
- hot_table: bfloat16 [4096, 128], replicated, may hold values from -3 to 3
- labels: int32 [4096], P(('grp', 'dev')), may hold values 0 or 1
- cross_u: bfloat16 [1664, 256], replicated, may hold values from -0.15625 to 0.15625
- cross_v: bfloat16 [256, 1664], replicated, may hold values from -0.375 to 0.375
- cross_bias: float32 [1664], replicated, may hold values from -3 to 3
- mlp_weight: bfloat16 [2048, 1664], replicated, may hold values from -0.15625 to 0.15625
- mlp_bias: float32 [2048], replicated, may hold values from -3 to 3
- out_weight: bfloat16 [2048], replicated, may hold values from -0.125 to 0.125
Outputs:
- cold_grad: float32 [65536, 128], P(('grp', 'dev'))
- hot_grad: float32 [4096, 128], replicated
- mlp_weight_grad: float32 [2048, 1664], P(('grp', 'dev'))
- cross_u_grad: float32 [1664, 256], replicated
- cross_v_grad: float32 [256, 1664], replicated
- cross_bias_grad: float32 [1664], replicated
- mlp_bias_grad: float32 [2048], replicated
- out_weight_grad: float32 [2048], replicated
The draws below stay inside these ranges and needn't reach their ends.
Inputs may be any that keep to these rules, and one draw needn't show every extreme that they name: The owner of an id is location[id] // 2048. Among the ids of one device's 128 samples (an aligned block of rows), at most 156 have any one owner; in every draw one owner has exactly 156 in every block. `location`: A permutation of 0 to 65535. `hot_list`: the 32 entries of each row are different.
All inputs are finite; a program needn't handle non-finite values. No bound on the sum of `labels` on one device may be relied on, other than what follows from the above.
Results may differ from the reference program's by a relative error of at most 0.0067.
Values may be sent and summed in bfloat16 or wider, within the bound.
A program may use at most 128 MiB of HBM per device.

```python
import jax
import jax.numpy as jnp
from jax import lax

E = 128
F = 13
HOTS = 2
R = 256
H = 2048
HOT_ROWS = 4096
HOT_DEV = 32
SAMP_DEV = 128
SHARD_ROWS = 2048
DIN = 1664
SAMPLES = 4096
ROWS = 65536


def route_tables(key):
    devices = SAMPLES // SAMP_DEV
    per_device = SAMP_DEV * F * HOTS
    mean_load = per_device // devices
    spread = mean_load // 2
    place_key, owner_key, device_key = jax.random.split(jax.random.fold_in(key, 7), 3)
    location = jax.random.permutation(place_key, ROWS).astype(jnp.int32)
    inverse = jnp.zeros((ROWS,), jnp.int32).at[location].set(jnp.arange(ROWS, dtype=jnp.int32))
    full_owner = jax.random.randint(owner_key, (), 0, devices).astype(jnp.int32)

    def one_device(single_key):
        pair_key, diff_key, shuffle_key, slot_key = jax.random.split(single_key, 4)
        ranking = jax.random.permutation(pair_key, devices).astype(jnp.int32)
        leading = ranking[0]
        ranking = jnp.where(ranking == full_owner, leading, ranking).at[0].set(full_owner)
        offsets = jax.random.randint(diff_key, (devices // 2,), 0, spread + 1).astype(jnp.int32).at[0].set(spread)
        paired = jnp.stack([mean_load + offsets, mean_load - offsets], axis=1).reshape(devices)
        counts = jnp.zeros((devices,), jnp.int32).at[ranking].set(paired)
        owners = jnp.repeat(jnp.arange(devices, dtype=jnp.int32), counts, total_repeat_length=per_device)
        owners = jax.random.permutation(shuffle_key, owners)
        row_slot = jax.random.randint(slot_key, (per_device,), 0, SHARD_ROWS).astype(jnp.int32)
        return inverse[owners * SHARD_ROWS + row_slot]
    ids = jax.vmap(one_device)(jax.random.split(device_key, devices))
    return (location, ids.reshape(SAMPLES, F, HOTS).astype(jnp.int32))


def draw_ids(key, part):
    return route_tables(key)[1]


def draw_location(key, part):
    return route_tables(key)[0]


def draw_hot_list(key, part):
    devices = SAMPLES // SAMP_DEV
    row_keys = jax.random.split(jax.random.fold_in(key, 11), devices)

    def pick_rows(single_key):
        return jax.random.permutation(single_key, HOT_ROWS)[:HOT_DEV]
    return jax.vmap(pick_rows)(row_keys).astype(jnp.int32)


def touch_ends(drawn, stream_key, least, largest):
    shape = drawn.shape
    place = [jax.random.randint(jax.random.fold_in(stream_key, axis), (), 0, shape[axis]) for axis in range(len(shape))]
    drawn = drawn.at[tuple(place)].set(least)
    longest = shape.index(max(shape))
    place[longest] = (place[longest] + 1) % shape[longest]
    return drawn.at[tuple(place)].set(largest)


def block_levels(rng, extent, cuts, smallest, top_value):
    factor_of = 1.0
    for dim, shards_of in cuts:
        heights = jax.random.uniform(jax.random.fold_in(jax.random.fold_in(rng, 6), dim), (shards_of,), jnp.float32, smallest / len(cuts), top_value / len(cuts))
        factor_of = factor_of * jnp.repeat(jnp.exp(heights), extent[dim] // shards_of).reshape((-1,) + (1,) * (len(extent) - 1 - dim))
    return factor_of


def bell_draw(stream_key, dims, width, reach, shards=(), kind=jnp.bfloat16):
    drawn = width * jax.random.normal(stream_key, dims, jnp.float32)
    if shards:
        drawn = drawn * block_levels(stream_key, dims, shards, -0.22, 0.18)
    return jnp.clip(drawn, -reach, reach).astype(kind)


def setup_inputs(seed: int = 0) -> dict:
    streams_of = jax.random.split(jax.random.key(seed), 14)
    return {
        "ids": draw_ids(jax.random.fold_in(streams_of[13], 71), 0),
        "location": draw_location(jax.random.fold_in(streams_of[13], 71), 0),
        "cold_table": bell_draw(streams_of[2], (ROWS, E), 0.5, 3.0, ((0, 32),)),
        "hot_index": touch_ends(jax.random.randint(streams_of[3], (SAMPLES, F), 0, HOT_DEV), jax.random.fold_in(streams_of[3], 1), 0, HOT_DEV - 1).astype(jnp.int32),
        "hot_list": draw_hot_list(jax.random.fold_in(streams_of[13], 71), 0),
        "hot_table": bell_draw(streams_of[5], (HOT_ROWS, E), 0.5, 3.0),
        "labels": touch_ends((jax.random.randint(streams_of[6], (SAMPLES,), 0, 4) < 1).astype(jnp.int32), jax.random.fold_in(streams_of[6], 1), 0, 1),
        "cross_u": bell_draw(streams_of[7], (DIN, R), DIN ** -0.5, 0.15625),
        "cross_v": bell_draw(streams_of[8], (R, DIN), R ** -0.5, 0.375),
        "cross_bias": bell_draw(streams_of[9], (DIN,), 0.5, 3.0, (), jnp.float32),
        "mlp_weight": bell_draw(streams_of[10], (H, DIN), DIN ** -0.5, 0.15625),
        "mlp_bias": bell_draw(streams_of[11], (H,), 0.5, 3.0, (), jnp.float32),
        "out_weight": bell_draw(streams_of[12], (H,), H ** -0.5, 0.125),
    }


def silu_slope(values):
    squash = jax.nn.sigmoid(values)
    return squash * (1.0 + values * (1.0 - squash))


def contract_rows(former, latter):
    return lax.dot_general(former, latter, (((0,), (0,)), ((), ())), preferred_element_type=jnp.float32)


def contract_cols(former, latter):
    return lax.dot_general(former, latter, (((1,), (1,)), ((), ())), preferred_element_type=jnp.float32)


def reference(ids, location, cold_table, hot_index, hot_list, hot_table, labels, cross_u, cross_v, cross_bias, mlp_weight, mlp_bias, out_weight):
    blocks = SAMPLES // SAMP_DEV
    placed = location[ids].astype(jnp.int32)
    inputs = (placed.reshape(blocks, SAMP_DEV, F, HOTS), hot_index.reshape(blocks, SAMP_DEV, F), labels.reshape(blocks, SAMP_DEV), hot_list)

    def one_block(carried, pieces):
        block_place, block_index, block_label, block_list = pieces
        cold_rows = cold_table[block_place].astype(jnp.float32)
        pooled = jnp.sum(cold_rows, axis=2)
        hot_rows = block_list[block_index]
        pooled = pooled + hot_table[hot_rows].astype(jnp.float32)
        first_input = pooled.reshape(SAMP_DEV, F * E).astype(jnp.bfloat16)
        cross_low = jnp.dot(first_input, cross_u, preferred_element_type=jnp.float32).astype(jnp.bfloat16)
        cross_term = jnp.dot(cross_low, cross_v, preferred_element_type=jnp.float32) + cross_bias
        input_wide = first_input.astype(jnp.float32)
        cross_out = (input_wide * cross_term + input_wide).astype(jnp.bfloat16)
        hidden_in = contract_cols(cross_out, mlp_weight) + mlp_bias
        hidden = jax.nn.silu(hidden_in).astype(jnp.bfloat16)
        logits = jnp.dot(hidden, out_weight, preferred_element_type=jnp.float32)
        logit_grad = jax.nn.sigmoid(logits) - block_label.astype(jnp.float32)
        out_grad = jnp.dot(logit_grad, hidden.astype(jnp.float32), precision=lax.Precision.HIGHEST)
        hidden_grad = (logit_grad[:, None] * out_weight.astype(jnp.float32)[None, :] * silu_slope(hidden_in)).astype(jnp.bfloat16)
        bias_grad = jnp.sum(hidden_grad.astype(jnp.float32), axis=0)
        weight_grad = contract_rows(hidden_grad, cross_out)
        cross_out_grad = jnp.dot(hidden_grad, mlp_weight, preferred_element_type=jnp.float32)
        term_grad = (cross_out_grad * input_wide).astype(jnp.bfloat16)
        cross_bias_part = jnp.sum(term_grad.astype(jnp.float32), axis=0)
        cross_v_part = contract_rows(cross_low, term_grad)
        low_grad = contract_cols(term_grad, cross_v).astype(jnp.bfloat16)
        cross_u_part = contract_rows(first_input, low_grad)
        pooled_grad = (cross_out_grad * (cross_term + 1.0) + contract_cols(low_grad, cross_u)).astype(jnp.bfloat16)
        grad_wide = pooled_grad.astype(jnp.float32).reshape(SAMP_DEV, F, E)
        spread_rows = jnp.broadcast_to(grad_wide[:, :, None, :], (SAMP_DEV, F, HOTS, E)).reshape(SAMP_DEV * F * HOTS, E)
        cold_next = carried[6].at[block_place.reshape(SAMP_DEV * F * HOTS)].add(spread_rows)
        hot_next = carried[7].at[hot_rows.reshape(SAMP_DEV * F)].add(grad_wide.reshape(SAMP_DEV * F, E))
        updated = (carried[0] + cross_u_part, carried[1] + cross_v_part, carried[2] + cross_bias_part, carried[3] + bias_grad, carried[4] + out_grad, carried[5] + weight_grad, cold_next, hot_next)
        return updated, None

    initial = (jnp.zeros((F * E, R), jnp.float32), jnp.zeros((R, F * E), jnp.float32), jnp.zeros((F * E,), jnp.float32), jnp.zeros((H,), jnp.float32), jnp.zeros((H,), jnp.float32), jnp.zeros((H, F * E), jnp.float32), jnp.zeros((ROWS, E), jnp.float32), jnp.zeros((HOT_ROWS, E), jnp.float32))
    totals = lax.scan(one_block, initial, inputs)[0]
    return (totals[6], totals[7], totals[5], totals[0], totals[1], totals[2], totals[3], totals[4])
```

```python
import functools
import math

import jax
import jax.numpy as jnp
from jax import lax
from jax.experimental import pallas as pl
from jax.experimental.pallas import tpu as pltpu
from jax.sharding import PartitionSpec as P

BOTH = ("grp", "dev")


def digits_of(values, limit):
    parts = []
    while limit > 1:
        parts.append(values % 256)
        values = values // 256
        limit = -(-limit // 256)
    return parts


def look_up(table, index):
    size = table.shape[0]
    lanes = 128
    rows = size // lanes
    parts = digits_of(table.reshape(rows, lanes), size)
    stacked = jnp.concatenate(parts, axis=1).astype(jnp.bfloat16)
    pick = (index[:, None] // lanes == jnp.arange(rows, dtype=jnp.int32)[None, :]).astype(jnp.bfloat16)
    found = jnp.dot(pick, stacked, preferred_element_type=jnp.float32)
    lane = (index[:, None] % lanes) == jnp.arange(lanes, dtype=jnp.int32)[None, :]
    total = 0.0
    for place in range(len(parts)):
        total = total + found[:, place * lanes : (place + 1) * lanes] * float(256**place)
    return jnp.sum(jnp.where(lane, total, 0.0), axis=1).astype(jnp.int32)


def rank_among(member, block):
    count, width = member.shape
    pieces = member.reshape(count // block, block, width)
    below = jnp.tril(jnp.ones((block, block), jnp.bfloat16), -1)
    inner = jnp.einsum("ij,bjd->bid", below, pieces, preferred_element_type=jnp.float32)
    sums = jnp.sum(pieces.astype(jnp.float32), axis=1)
    over = jnp.tril(jnp.ones((count // block, count // block), jnp.bfloat16), -1)
    outer = jnp.dot(over, sums.astype(jnp.bfloat16), preferred_element_type=jnp.float32)
    return (inner + outer[:, None, :]).reshape(count, width)


def select_rows(index, table):
    pick = index[:, None] == jnp.arange(table.shape[0], dtype=jnp.int32)[None, :]
    return jnp.dot(pick.astype(table.dtype), table, preferred_element_type=jnp.float32).astype(table.dtype)


def add_rows_kernel(index_ref, grad_ref, out_ref):
    @pl.when(pl.program_id(0) == 0)
    def _():
        out_ref[...] = jnp.zeros_like(out_ref)

    chunk = grad_ref.shape[0]
    rows = out_ref.shape[0]
    step = 256
    index = index_ref[0]
    grads = grad_ref[...]
    for first in range(0, rows, step):
        pick = lax.broadcasted_iota(jnp.int32, (step, chunk), 0) + first == index
        pick = jnp.where(pick, 1.0, 0.0).astype(jnp.bfloat16)
        out_ref[first : first + step, :] += jnp.dot(pick, grads, preferred_element_type=jnp.float32)


def add_rows(index, grads, rows):
    count, width = grads.shape
    chunk = 512 if count % 512 == 0 else count
    return pl.pallas_call(
        add_rows_kernel,
        grid=(count // chunk,),
        in_specs=[
            pl.BlockSpec((1, 1, chunk), lambda step: (step, 0, 0)),
            pl.BlockSpec((chunk, width), lambda step: (step, 0)),
        ],
        out_specs=pl.BlockSpec((rows, width), lambda step: (0, 0)),
        out_shape=jax.ShapeDtypeStruct((rows, width), jnp.float32),
        cost_estimate=pl.CostEstimate(
            flops=2 * count * rows * width, bytes_accessed=count * width * 2 + rows * width * 4, transcendentals=0
        ),
    )(index.reshape(count // chunk, 1, chunk), grads)


def exchange_kernel(
    groups,
    stack,
    cut,
    mlp_ref,
    uv_ref,
    small_ref,
    grad_ref,
    held_ref,
    mlp_out,
    uv_out,
    small_out,
    cold_out,
    pair_mlp,
    pair_uv,
    sum_mlp,
    sum_uv,
    a_in_mlp,
    a_in_uv,
    b_in_mlp,
    b_in_uv,
    a_sum_mlp,
    a_sum_uv,
    b_sum_mlp,
    b_sum_uv,
    a_end_mlp,
    a_end_uv,
    b_end_mlp,
    b_end_uv,
    all_uv,
    all_small,
    cold_in,
    send_sem,
    recv_sem,
    grad_send,
    grad_recv,
):
    g = lax.axis_index("grp")
    d = lax.axis_index("dev")
    z = lax.div(d, 2)
    c = lax.rem(d, 2)
    width = mlp_ref.shape[-1]
    mesh_id = pl.DeviceIdType.MESH

    def turn(here, by, size):
        return lax.rem(here + by, size)

    barrier = pltpu.get_barrier_semaphore()
    devices = groups * stack * 2
    me = g * (stack * 2) + d
    capacity = grad_ref.shape[1]

    def spot(flat):
        return (lax.div(flat, stack * 2), lax.rem(flat, stack * 2))

    @pl.loop(1, devices)
    def _(k):
        pl.semaphore_signal(barrier, inc=1, device_id=spot(turn(me, k, devices)), device_id_type=mesh_id)

    pl.semaphore_wait(barrier, devices - 1)
    own_rows = pl.ds(pl.multiple_of(me * capacity, 16), capacity)

    def hand(k):
        return pltpu.make_async_remote_copy(
            src_ref=grad_ref.at[turn(me, k, devices)],
            dst_ref=cold_in.at[own_rows],
            send_sem=grad_send.at[k],
            recv_sem=grad_recv.at[k],
            device_id=spot(turn(me, k, devices)),
            device_id_type=mesh_id,
        )

    started = []

    def send(source, target, to_g, to_z, to_c):
        place = len(started)
        copy = pltpu.make_async_remote_copy(
            src_ref=source,
            dst_ref=target,
            send_sem=send_sem.at[place],
            recv_sem=recv_sem.at[place],
            device_id=(to_g, to_z * 2 + to_c),
            device_id_type=mesh_id,
        )
        copy.start()
        started.append(copy)
        return copy

    def landed(copies):
        for copy in copies:
            copy.wait_recv()

    def wide(value):
        return value.astype(jnp.float32)

    both = ((mlp_ref, pair_mlp, sum_mlp), (uv_ref, pair_uv, sum_uv))
    a_refs = ((sum_mlp, a_in_mlp, a_sum_mlp, a_end_mlp), (sum_uv, a_in_uv, a_sum_uv, a_end_uv))
    b_refs = ((sum_mlp, b_in_mlp, b_sum_mlp, b_end_mlp), (sum_uv, b_in_uv, b_sum_uv, b_end_uv))
    left, right = slice(0, cut), slice(cut, width)

    order = [turn(g, k, groups) for k in range(1, groups)] + [g]
    crossing = [
        [send(full.at[block, :, 1 - c], pair.at[block], g, z, 1 - c) for full, pair, _ in both] for block in order
    ]
    small_z = [
        send(small_ref, all_small.at[g, z, c], g, turn(z, k, stack), c) for k in range(1, stack)
    ]
    all_small[g, z, c] = small_ref[...]

    @pl.loop(1, devices)
    def _(k):
        hand(k).start()

    cold_in[own_rows, :] = grad_ref[me]
    cold_out[...] = jnp.zeros_like(cold_out)
    b_first = []
    for k, block in enumerate(order):
        landed(crossing[k])
        for full, pair, total in both:

            @pl.loop(0, stack)
            def _(level, full=full, pair=pair, total=total, block=block):
                total[block, level] = (wide(full[block, level, c]) + wide(pair[block, level])).astype(total.dtype)

        if k < groups - 1:
            for total, arrived, _, _ in b_refs:
                b_first.append(send(total.at[block, :, :, right], arrived.at[k], block, z, c))
    a_first = []
    for k in range(1, stack):
        to_z = turn(z, k, stack)
        for total, arrived, _, _ in a_refs:
            a_first.append(send(total.at[:, to_z, :, left], arrived.at[k - 1], g, to_z, c))

    landed(small_z)
    small_g = [
        send(all_small.at[g, :, c], all_small.at[g, :, c], turn(g, k, groups), z, c) for k in range(1, groups)
    ]


    @pl.loop(1, devices)
    def _(k):
        hand(k).wait_recv()

    chunk = held_ref.shape[-1]
    step = 256

    @pl.loop(0, held_ref.shape[0])
    def _(piece):
        index = held_ref[piece]
        grads = cold_in[pl.ds(pl.multiple_of(piece * chunk, 16), chunk), :]
        for first in range(0, cold_out.shape[0], step):
            pick = lax.broadcasted_iota(jnp.int32, (step, chunk), 0) + first == index
            pick = jnp.where(pick, 1.0, 0.0).astype(jnp.bfloat16)
            cold_out[first : first + step, :] += jnp.dot(pick, grads, preferred_element_type=jnp.float32)

    landed(b_first)
    for total, arrived, partial, _ in b_refs:

        @pl.loop(0, stack)
        def _(level, total=total, arrived=arrived, partial=partial):
            value = wide(total[g, level, :, right])
            for k in range(groups - 1):
                value = value + wide(arrived[k, level])
            partial[level] = value.astype(partial.dtype)

    b_last = []
    for k in range(1, stack):
        to_z = turn(z, k, stack)
        for _, _, partial, ending in b_refs:
            b_last.append(send(partial.at[to_z], ending.at[k - 1], g, to_z, c))

    landed(a_first)
    for total, arrived, partial, _ in a_refs:

        @pl.loop(0, groups)
        def _(block, total=total, arrived=arrived, partial=partial):
            value = wide(total[block, z, :, left])
            for k in range(stack - 1):
                value = value + wide(arrived[k, block])
            partial[block] = value.astype(partial.dtype)

    a_last = []
    for k in range(1, groups):
        to_g = turn(g, k, groups)
        for _, _, partial, ending in a_refs:
            a_last.append(send(partial.at[to_g], ending.at[k - 1], to_g, z, c))

    landed(small_g)
    small_c = [send(all_small.at[:, :, c], all_small.at[:, :, c], g, z, 1 - c)]

    landed(b_last)
    for place, (_, _, partial, ending) in enumerate(b_refs):
        value = wide(partial[z])
        for k in range(stack - 1):
            value = value + wide(ending[k])
        if place == 0:
            mlp_out[:, right] = value
        else:
            all_uv[g, z, c, :, right] = value.astype(all_uv.dtype)
    landed(a_last)
    for place, (_, _, partial, ending) in reversed(list(enumerate(a_refs))):
        value = wide(partial[g])
        for k in range(groups - 1):
            value = value + wide(ending[k])
        if place == 1:
            all_uv[g, z, c, :, left] = value.astype(all_uv.dtype)
        else:
            mlp_out[:, left] = value

    own = all_uv.at[g, z, c]
    landed([send(own, own, g, turn(z, k, stack), c) for k in range(1, stack)])
    column = all_uv.at[g, :, c]
    landed([send(column, column, turn(g, k, groups), z, c) for k in range(1, groups)])
    parity = all_uv.at[:, :, c]
    landed([send(parity, parity, g, z, 1 - c)])
    landed(small_c)
    for source, target in ((all_uv, uv_out), (all_small, small_out)):

        @pl.loop(0, groups)
        def _(block, source=source, target=target):
            @pl.loop(0, stack)
            def _(level):
                for core in range(2):
                    target[block, level, core] = source[block, level, core]

    for copy in started:
        copy.wait_send()

    @pl.loop(1, devices)
    def _(k):
        hand(k).wait_send()


def exchange(mlp_part, uv_part, small, grads, held_slot, shard_rows):
    groups = lax.axis_size("grp")
    stack = lax.axis_size("dev") // 2
    devices = groups * stack * 2
    width = mlp_part.shape[1]
    rows = mlp_part.shape[0] // devices
    uv_rows = uv_part.shape[0] // devices
    cut = max(width // 512, 1) * 128
    rest = width - cut
    half = jnp.bfloat16
    sizes = (rows, uv_rows)
    scratch = []
    scratch += [pltpu.VMEM((groups, stack, size, width), half) for size in sizes]
    scratch += [pltpu.VMEM((groups, stack, size, width), half) for size in sizes]
    scratch += [pltpu.VMEM((stack - 1, groups, size, cut), half) for size in sizes]
    scratch += [pltpu.VMEM((groups - 1, stack, size, rest), half) for size in sizes]
    scratch += [pltpu.VMEM((groups, size, cut), half) for size in sizes]
    scratch += [pltpu.VMEM((stack, size, rest), half) for size in sizes]
    scratch += [pltpu.VMEM((groups - 1, size, cut), half) for size in sizes]
    scratch += [pltpu.VMEM((stack - 1, size, rest), half) for size in sizes]
    lead = (groups, stack, 2)
    scratch += [pltpu.VMEM(lead + (uv_rows, width), half), pltpu.VMEM(lead + small.shape, small.dtype)]
    copies = 2 * groups + 6 * (stack - 1) + 6 * (groups - 1) + 2
    count, grad_width = devices * grads.shape[1], grads.shape[2]
    chunk = 512 if count % 512 == 0 else count
    scratch += [pltpu.VMEM((count, grad_width), half)]
    scratch += [pltpu.SemaphoreType.DMA((copies,))] * 2 + [pltpu.SemaphoreType.DMA((devices,))] * 2
    whole = pl.BlockSpec(memory_space=pltpu.VMEM)
    sent = mlp_part.size * 2 + uv_part.size * 2
    held = sum(math.prod(ref.shape) * jnp.dtype(ref.dtype).itemsize for ref in scratch[:-4])
    held += sent + rows * width * 4 + uv_part.size * 2 + (devices + 1) * small.size * 4
    held += count * grad_width * 2 + shard_rows * grad_width * 4 + count * 32
    limit = min(held + 4 * 1024 * 1024, 61 * 1024 * 1024)
    mlp_sum, uv_sum, every_small, cold_grad = pl.pallas_call(
        functools.partial(exchange_kernel, groups, stack, cut),
        in_specs=[whole] * 5,
        out_specs=[whole] * 4,
        out_shape=[
            jax.ShapeDtypeStruct((rows, width), jnp.float32),
            jax.ShapeDtypeStruct(lead + (uv_rows, width), half),
            jax.ShapeDtypeStruct(lead + small.shape, small.dtype),
            jax.ShapeDtypeStruct((shard_rows, grad_width), jnp.float32),
        ],
        scratch_shapes=scratch,
        compiler_params=pltpu.CompilerParams(
            collective_id=0, has_side_effects=True, vmem_limit_bytes=limit
        ),
        cost_estimate=pl.CostEstimate(flops=0, bytes_accessed=16 * sent, transcendentals=0),
    )(
        mlp_part.reshape(lead + (rows, width)),
        uv_part.reshape(lead + (uv_rows, width)),
        small,
        grads,
        held_slot.reshape(count // chunk, 1, chunk),
    )
    return mlp_sum, uv_sum.reshape(devices * uv_rows, width), every_small.reshape((devices,) + small.shape), cold_grad


def fetch_kernel(
    devices,
    slot_ref,
    place_ref,
    base_ref,
    table_ref,
    out_ref,
    asked_ref,
    asked,
    found,
    arrived,
    total,
    ask_send,
    ask_recv,
    row_send,
    row_recv,
):
    per_group = lax.axis_size("dev")
    me = lax.axis_index("grp") * per_group + lax.axis_index("dev")
    mesh_id = pl.DeviceIdType.MESH
    capacity = slot_ref.shape[-1]
    shard_rows, row_width = table_ref.shape
    pairs, bags = place_ref.shape
    samples = out_ref.shape[0]

    def spot(flat):
        return (lax.div(flat, per_group), lax.rem(flat, per_group))

    def after(k):
        return lax.rem(me + k, devices)

    def before(k):
        return lax.rem(me + devices - k, devices)

    def ask(k):
        return pltpu.make_async_remote_copy(
            src_ref=slot_ref.at[after(k)],
            dst_ref=asked.at[me],
            send_sem=ask_send.at[k],
            recv_sem=ask_recv.at[k],
            device_id=spot(after(k)),
            device_id_type=mesh_id,
        )

    def answer(k):
        return pltpu.make_async_remote_copy(
            src_ref=found.at[before(k)],
            dst_ref=arrived.at[me],
            send_sem=row_send.at[k],
            recv_sem=row_recv.at[k],
            device_id=spot(before(k)),
            device_id_type=mesh_id,
        )

    barrier = pltpu.get_barrier_semaphore()

    @pl.loop(1, devices)
    def _(k):
        pl.semaphore_signal(barrier, inc=1, device_id=spot(after(k)), device_id_type=mesh_id)

    pl.semaphore_wait(barrier, devices - 1)

    @pl.loop(1, devices)
    def _(k):
        ask(k).start()

    asked[me] = slot_ref[me]
    total[...] = base_ref[...]

    square = (capacity, capacity)
    diagonal = lax.broadcasted_iota(jnp.int32, square, 0) == lax.broadcasted_iota(jnp.int32, square, 1)

    def rows_for(owner_of):
        wish = asked[owner_of].astype(jnp.float32)
        column = jnp.sum(jnp.where(diagonal, wish, 0.0), axis=1, keepdims=True).astype(jnp.int32) - 1
        value = jnp.zeros((capacity, row_width), jnp.float32)
        step = 512
        for first in range(0, shard_rows, step):
            pick = lax.broadcasted_iota(jnp.int32, (capacity, step), 1) + first == column
            pick = jnp.where(pick, 1.0, 0.0).astype(jnp.bfloat16)
            value = value + jnp.dot(
                pick, table_ref[first : first + step, :], preferred_element_type=jnp.float32
            )
        return value.astype(jnp.bfloat16)

    @pl.loop(1, devices)
    def _(k):
        ask(k).wait_recv()
        found[before(k)] = rows_for(before(k))
        answer(k).start()

    arrived[me] = rows_for(me)

    chunk = pairs // 4

    def gather_in(source):
        rows = arrived[source]
        for first in range(0, pairs, chunk):
            places = place_ref[first : first + chunk, :] - source * capacity
            lane = lax.broadcasted_iota(jnp.int32, (chunk, capacity), 1)
            hit = lane == places[:, 0:1]
            for bag in range(1, bags):
                hit = hit | (lane == places[:, bag : bag + 1])
            hit = jnp.where(hit, 1.0, 0.0).astype(jnp.bfloat16)
            total[first : first + chunk, :] += jnp.dot(hit, rows, preferred_element_type=jnp.float32)

    gather_in(me)

    @pl.loop(1, devices)
    def _(k):
        answer(k).wait_recv()
        gather_in(after(k))

    for feature in range(pairs // samples):
        out_ref[:, feature * row_width : (feature + 1) * row_width] = total[
            feature * samples : (feature + 1) * samples, :
        ].astype(out_ref.dtype)
    asked_ref[...] = asked[...]

    @pl.loop(1, devices)
    def _(k):
        ask(k).wait_send()
        answer(k).wait_send()


def fetch(slots, places, base, table, samples):
    devices, capacity = slots.shape
    pairs, row_width = base.shape
    whole = pl.BlockSpec(memory_space=pltpu.VMEM)
    block = (devices, capacity, row_width)
    first_input, asked = pl.pallas_call(
        functools.partial(fetch_kernel, devices),
        in_specs=[whole] * 4,
        out_specs=[whole] * 2,
        out_shape=[
            jax.ShapeDtypeStruct((samples, pairs // samples * row_width), jnp.bfloat16),
            jax.ShapeDtypeStruct((devices, 1, capacity), jnp.int32),
        ],
        scratch_shapes=[
            pltpu.VMEM((devices, 1, capacity), jnp.int32),
            pltpu.VMEM(block, jnp.bfloat16),
            pltpu.VMEM(block, jnp.bfloat16),
            pltpu.VMEM((pairs, row_width), jnp.float32),
        ]
        + [pltpu.SemaphoreType.DMA((devices,))] * 4,
        compiler_params=pltpu.CompilerParams(
            collective_id=1, has_side_effects=True, vmem_limit_bytes=32 * 1024 * 1024
        ),
    )(slots.reshape(devices, 1, capacity), places, base, table)
    return first_input, asked.reshape(devices, capacity)


def silu_slope(values):
    squash = jax.nn.sigmoid(values)
    return squash * (1.0 + values * (1.0 - squash))


def contract_rows(former, latter):
    return lax.dot_general(
        former, latter, (((0,), (0,)), ((), ())), preferred_element_type=jnp.float32
    )


def contract_cols(former, latter):
    return lax.dot_general(
        former, latter, (((1,), (1,)), ((), ())), preferred_element_type=jnp.float32
    )


def per_device(
    ids,
    location,
    cold_table,
    hot_index,
    hot_list,
    hot_table,
    labels,
    cross_u,
    cross_v,
    cross_bias,
    mlp_weight,
    mlp_bias,
    out_weight,
):
    devices = lax.axis_size(BOTH)
    samples, features, bag_size = ids.shape
    shard_rows, row_width = cold_table.shape
    pairs = samples * features
    requests = pairs * bag_size
    mean_load = requests // devices
    capacity = -(-(mean_load + mean_load // 2) // 16) * 16
    placed = look_up(location, ids.transpose(2, 1, 0).reshape(requests))
    owners = placed // shard_rows
    row_slot = placed - owners * shard_rows
    by_owner = owners[:, None] == jnp.arange(devices, dtype=jnp.int32)[None, :]
    member = by_owner.astype(jnp.bfloat16)
    counted = rank_among(member, samples)
    rank = jnp.sum(jnp.where(by_owner, counted, 0.0), axis=1).astype(jnp.int32)
    position = owners * capacity + rank
    ranked = rank[:, None] == jnp.arange(capacity, dtype=jnp.int32)[None, :]
    pair = jnp.arange(requests, dtype=jnp.int32) % pairs
    tables = digits_of(row_slot + 1, shard_rows + 1)
    cut = len(tables)
    tables = tables + digits_of(pair, pairs)
    sheet = jnp.concatenate(
        [jnp.where(ranked, part.astype(jnp.float32)[:, None], 0.0) for part in tables], axis=1
    ).astype(jnp.bfloat16)
    laid = contract_rows(member, sheet).astype(jnp.int32)

    def joined(first, last):
        total = 0
        for place in range(first, last):
            total = total + laid[:, place * capacity : (place + 1) * capacity] * (256 ** (place - first))
        return total

    send_slot = joined(0, cut)
    source = joined(cut, len(tables)).reshape(devices * capacity)
    hot_slots = hot_list.shape[1]
    hot_flat = hot_index.transpose(1, 0).reshape(pairs)
    selector = (hot_flat[:, None] == jnp.arange(hot_slots, dtype=jnp.int32)[None, :]).astype(jnp.bfloat16)
    pooled = jnp.dot(selector, hot_table[hot_list[0]], preferred_element_type=jnp.float32)
    places = position.reshape(bag_size, pairs).transpose(1, 0)
    first_input, wanted = fetch(send_slot, places, pooled, cold_table, samples)
    held_slot = wanted.reshape(devices * capacity) - 1
    cross_low = jnp.dot(first_input, cross_u, preferred_element_type=jnp.float32).astype(
        jnp.bfloat16
    )
    cross_term = jnp.dot(cross_low, cross_v, preferred_element_type=jnp.float32) + cross_bias
    input_wide = first_input.astype(jnp.float32)
    cross_out = (input_wide * cross_term + input_wide).astype(jnp.bfloat16)
    hidden_in = contract_cols(cross_out, mlp_weight) + mlp_bias
    hidden = jax.nn.silu(hidden_in).astype(jnp.bfloat16)
    logits = jnp.dot(hidden, out_weight, preferred_element_type=jnp.float32)
    logit_grad = jax.nn.sigmoid(logits) - labels.astype(jnp.float32)
    out_grad = jnp.dot(logit_grad, hidden.astype(jnp.float32), precision=lax.Precision.HIGHEST)
    hidden_grad = (
        logit_grad[:, None] * out_weight.astype(jnp.float32)[None, :] * silu_slope(hidden_in)
    ).astype(jnp.bfloat16)
    bias_grad = jnp.sum(hidden_grad.astype(jnp.float32), axis=0)
    mlp_part = contract_rows(hidden_grad, cross_out).astype(jnp.bfloat16)
    cross_out_grad = jnp.dot(hidden_grad, mlp_weight, preferred_element_type=jnp.float32)
    term_grad = (cross_out_grad * input_wide).astype(jnp.bfloat16)
    cross_bias_part = jnp.sum(term_grad.astype(jnp.float32), axis=0)
    cross_v_part = contract_rows(cross_low, term_grad)
    low_grad = contract_cols(term_grad, cross_v).astype(jnp.bfloat16)
    cross_u_part = contract_rows(low_grad, first_input)
    pooled_grad = (cross_out_grad * (cross_term + 1.0) + contract_cols(low_grad, cross_u)).astype(
        jnp.bfloat16
    )
    pair_grad = pooled_grad.reshape(samples, features, row_width).transpose(1, 0, 2).reshape(pairs, row_width)
    send_grad = select_rows(source, pair_grad).reshape(devices, capacity, row_width)
    hot_block = contract_rows(selector, pair_grad)
    rank_width, in_width = cross_v.shape
    uv_part = jnp.concatenate([cross_u_part, cross_v_part], axis=0).astype(jnp.bfloat16)
    uv_pad = -uv_part.shape[0] % (16 * devices)
    uv_part = jnp.pad(uv_part, ((0, uv_pad), (0, 0)))
    listed = jnp.pad(hot_list[0].astype(jnp.float32), (0, -hot_slots % row_width))
    list_width = listed.shape[0]
    sums = jnp.concatenate([listed, cross_bias_part, bias_grad, out_grad])
    hidden_width = bias_grad.shape[0]
    sums = jnp.pad(sums, (0, -sums.shape[0] % (8 * row_width))).reshape(-1, row_width)
    small = jnp.concatenate([hot_block, sums], axis=0)
    mlp_weight_grad, uv_sum, every_small, cold_grad = exchange(
        mlp_part, uv_part, small, send_grad, held_slot, shard_rows
    )
    every_block = every_small[:, :hot_slots].astype(jnp.bfloat16).reshape(devices * hot_slots, row_width)
    every_sum = every_small[:, hot_slots:].reshape(devices, -1)
    every_row = every_sum[:, :hot_slots].astype(jnp.int32).reshape(devices * hot_slots)
    hot_grad = add_rows(every_row, every_block, hot_table.shape[0])
    added = jnp.sum(every_sum[:, list_width:], axis=0)
    cross_u_grad = uv_sum[:rank_width].transpose(1, 0).astype(jnp.float32)
    cross_v_grad = uv_sum[rank_width : 2 * rank_width].astype(jnp.float32)
    cross_bias_grad = added[:in_width]
    mlp_bias_grad = added[in_width : in_width + hidden_width]
    out_weight_grad = added[in_width + hidden_width : in_width + 2 * hidden_width]
    return (
        cold_grad,
        hot_grad,
        mlp_weight_grad,
        cross_u_grad,
        cross_v_grad,
        cross_bias_grad,
        mlp_bias_grad,
        out_weight_grad,
    )


def solution(mesh):
    placed = (
        P(("grp", "dev"), None, None),
        P(),
        P(("grp", "dev"), None),
        P(("grp", "dev"), None),
        P(("grp", "dev"), None),
        P(),
        P(("grp", "dev")),
        P(),
        P(),
        P(),
        P(),
        P(),
        P(),
    )
    return jax.shard_map(
        per_device,
        mesh=mesh,
        in_specs=placed,
        out_specs=(P(("grp", "dev"), None), P(), P(("grp", "dev"), None), P(), P(), P(), P(), P()),
        check_vma=False,
    )
```

```python
import functools
import math

import jax
import jax.numpy as jnp
from jax import lax
from jax.experimental import pallas as pl
from jax.experimental.pallas import tpu as pltpu
from jax.sharding import PartitionSpec as P

BOTH = ("grp", "dev")


def digits_of(values, limit):
    parts = []
    while limit > 1:
        parts.append(values % 256)
        values = values // 256
        limit = -(-limit // 256)
    return parts


def look_up(table, index):
    size = table.shape[0]
    lanes = 128
    rows = size // lanes
    parts = digits_of(table.reshape(rows, lanes), size)
    stacked = jnp.concatenate(parts, axis=1).astype(jnp.bfloat16)
    pick = (index[:, None] // lanes == jnp.arange(rows, dtype=jnp.int32)[None, :]).astype(jnp.bfloat16)
    found = jnp.dot(pick, stacked, preferred_element_type=jnp.float32)
    lane = (index[:, None] % lanes) == jnp.arange(lanes, dtype=jnp.int32)[None, :]
    total = 0.0
    for place in range(len(parts)):
        total = total + found[:, place * lanes : (place + 1) * lanes] * float(256**place)
    return jnp.sum(jnp.where(lane, total, 0.0), axis=1).astype(jnp.int32)


def rank_among(member, block):
    count, width = member.shape
    pieces = member.reshape(count // block, block, width)
    below = jnp.tril(jnp.ones((block, block), jnp.bfloat16), -1)
    inner = jnp.einsum("ij,bjd->bid", below, pieces, preferred_element_type=jnp.float32)
    sums = jnp.sum(pieces.astype(jnp.float32), axis=1)
    over = jnp.tril(jnp.ones((count // block, count // block), jnp.bfloat16), -1)
    outer = jnp.dot(over, sums.astype(jnp.bfloat16), preferred_element_type=jnp.float32)
    return (inner + outer[:, None, :]).reshape(count, width)


def add_rows_kernel(index_ref, grad_ref, out_ref):
    @pl.when(pl.program_id(0) == 0)
    def _():
        out_ref[...] = jnp.zeros_like(out_ref)

    chunk = grad_ref.shape[0]
    rows = out_ref.shape[0]
    step = 256
    index = index_ref[0]
    grads = grad_ref[...]
    for first in range(0, rows, step):
        pick = lax.broadcasted_iota(jnp.int32, (step, chunk), 0) + first == index
        pick = jnp.where(pick, 1.0, 0.0).astype(jnp.bfloat16)
        out_ref[first : first + step, :] += jnp.dot(pick, grads, preferred_element_type=jnp.float32)


def add_rows(index, grads, rows):
    count, width = grads.shape
    chunk = 512 if count % 512 == 0 else count
    return pl.pallas_call(
        add_rows_kernel,
        grid=(count // chunk,),
        in_specs=[
            pl.BlockSpec((1, 1, chunk), lambda step: (step, 0, 0)),
            pl.BlockSpec((chunk, width), lambda step: (step, 0)),
        ],
        out_specs=pl.BlockSpec((rows, width), lambda step: (0, 0)),
        out_shape=jax.ShapeDtypeStruct((rows, width), jnp.float32),
        cost_estimate=pl.CostEstimate(
            flops=2 * count * rows * width, bytes_accessed=count * width * 2 + rows * width * 4, transcendentals=0
        ),
    )(index.reshape(count // chunk, 1, chunk), grads)


def tiles(width, step=256):
    return [slice(first, min(first + step, width)) for first in range(0, width, step)]


def train_kernel(
    groups,
    stack,
    input_ref,
    cross_u_ref,
    cross_v_ref,
    cross_bias_ref,
    mlp_ref,
    mlp_bias_ref,
    out_weight_ref,
    label_ref,
    source_ref,
    held_ref,
    hot_ref,
    list_ref,
    mlp_out,
    uv_out,
    small_out,
    cold_out,
    term_buf,
    hidden_buf,
    squash_buf,
    active_buf,
    grad_buf,
    turned_buf,
    pool_buf,
    slope_buf,
    pair_buf,
    sums_buf,
    part_mlp,
    part_uv,
    grad_rows,
    outs_all,
    turned_all,
    pair_mlp,
    sum_mlp,
    end_mlp,
    pair_uv,
    sum_uv,
    in_uv,
    zsum_uv,
    end_uv,
    all_uv,
    all_small,
    cold_in,
    send_sem,
    recv_sem,
    row_send,
    row_recv,
):
    g = lax.axis_index("grp")
    d = lax.axis_index("dev")
    z = lax.div(d, 2)
    c = lax.rem(d, 2)
    half = jnp.bfloat16
    mesh_id = pl.DeviceIdType.MESH
    samples, width = input_ref.shape
    rank = cross_v_ref.shape[0]
    hidden_width = mlp_ref.shape[0]
    rows = mlp_out.shape[0]
    uv_rows = part_uv.shape[3]
    capacity = source_ref.shape[-1]
    pairs, row_width = pair_buf.shape
    hot_slots = all_small.shape[3] - sums_buf.shape[0]
    devices = groups * stack * 2
    me = g * (stack * 2) + d

    def turn(here, by, size):
        return lax.rem(here + by, size)

    def spot(flat):
        return (lax.div(flat, stack * 2), lax.rem(flat, stack * 2))

    def wide(value):
        return value.astype(jnp.float32)

    def dot(former, latter):
        return jnp.dot(former, latter, preferred_element_type=jnp.float32)

    def turned(value):
        return wide(value).T.astype(half)

    started = []

    def send(source, target, to_g, to_z, to_c):
        place = len(started)
        copy = pltpu.make_async_remote_copy(
            src_ref=source,
            dst_ref=target,
            send_sem=send_sem.at[place],
            recv_sem=recv_sem.at[place],
            device_id=(to_g, to_z * 2 + to_c),
            device_id_type=mesh_id,
        )
        copy.start()
        started.append(copy)
        return copy

    def landed(copies):
        for copy in copies:
            copy.wait_recv()

    def own_rows(flat):
        return pl.ds(pl.multiple_of(flat * capacity, 16), capacity)

    def hand(k):
        to = turn(me, k, devices)
        return pltpu.make_async_remote_copy(
            src_ref=grad_rows.at[to],
            dst_ref=cold_in.at[me],
            send_sem=row_send.at[k],
            recv_sem=row_recv.at[k],
            device_id=spot(to),
            device_id_type=mesh_id,
        )

    barrier = pltpu.get_barrier_semaphore()

    @pl.loop(1, devices)
    def _(k):
        pl.semaphore_signal(barrier, inc=1, device_id=spot(turn(me, k, devices)), device_id_type=mesh_id)

    low = dot(input_ref[...], cross_u_ref[...]).astype(half)
    for cols in tiles(width):
        term = dot(low, cross_v_ref[:, cols]) + cross_bias_ref[:, cols]
        value = wide(input_ref[:, cols])
        term_buf[:, cols] = term
        outs_all[g, :, cols] = (value * term + value).astype(half)

    pl.semaphore_wait(barrier, devices - 1)
    paired = groups == 4
    across = lax.div(g, 2) * 2 + 1 - lax.rem(g, 2)
    along = turn(g, 2, groups)
    middle = (width // row_width + 1) // 2 * row_width
    left, right = slice(0, middle), slice(middle, width)

    def send_outs(block, cols, to_g):
        piece = outs_all.at[block, :, cols]
        return send(piece, piece, to_g, z, c)

    if paired:
        outs_first = [send_outs(g, left, across), send_outs(g, right, along)]
        outs_sent = [send_outs(g, right, across), send_outs(g, left, along)]
    else:
        outs_sent = [send_outs(g, slice(0, width), turn(g, k, groups)) for k in range(1, groups)]

    score = jnp.zeros((samples, 1), jnp.float32)
    for cols in tiles(hidden_width):
        value = contract_cols(outs_all[g], mlp_ref[cols, :]) + mlp_bias_ref[:, cols]
        squash = jax.nn.sigmoid(value)
        active = (value * squash).astype(half)
        hidden_buf[:, cols] = value
        squash_buf[:, cols] = squash
        active_buf[:, cols] = active
        score = score + jnp.sum(wide(active) * out_weight_ref[:, cols], axis=1, keepdims=True)

    square = (samples, samples)
    diagonal = lax.broadcasted_iota(jnp.int32, square, 0) == lax.broadcasted_iota(jnp.int32, square, 1)
    label = jnp.sum(jnp.where(diagonal, wide(label_ref[...]), 0.0), axis=1, keepdims=True)
    score_grad = jax.nn.sigmoid(score) - label

    sums_buf[...] = jnp.zeros_like(sums_buf)
    sums_buf[0:2, :] = list_ref[...]

    def keep_sum(first, cols, value):
        start = first + cols.start // row_width
        for place in range(value.shape[1] // row_width):
            sums_buf[start + place : start + place + 1, :] = value[:, place * row_width : (place + 1) * row_width]

    bias_at = 2 + width // row_width
    out_at = bias_at + hidden_width // row_width
    share = hidden_width // groups
    for cols in tiles(hidden_width):
        value = hidden_buf[:, cols]
        squash = squash_buf[:, cols]
        slope = squash * (1.0 + value * (1.0 - squash))
        grad = (score_grad * out_weight_ref[:, cols] * slope).astype(half)
        grad_buf[:, cols] = grad
        keep_sum(bias_at, cols, jnp.sum(wide(grad), axis=0, keepdims=True))
        keep_sum(out_at, cols, jnp.sum(wide(active_buf[:, cols]) * score_grad, axis=0, keepdims=True))
        inside = cols.start % share
        turned_buf[cols.start // share, inside : inside + cols.stop - cols.start, :] = turned(grad)
    if paired:
        landed(outs_first)
        outs_sent += [send_outs(across, left, along), send_outs(along, right, across)]
    turned_sent = []
    for k in range(1, groups):
        to_g = turn(g, k, groups)
        turned_sent.append(send(turned_buf.at[to_g], turned_all.at[g], to_g, z, c))
    turned_all[g] = turned_buf[g]

    for cols in tiles(width):
        back = dot(grad_buf[...], mlp_ref[:, cols])
        slope = (back * wide(input_ref[:, cols])).astype(half)
        slope_buf[:, cols] = slope
        pool_buf[:, cols] = back * (term_buf[:, cols] + 1.0)
        keep_sum(2, cols, jnp.sum(wide(slope), axis=0, keepdims=True))

    def keep_uv(first, cols, part):
        for place in range(rank // uv_rows):
            flat = first // uv_rows + place
            block, level, core = flat // (stack * 2), flat // 2 % stack, flat % 2
            part_uv[block, level, core, :, cols] = part[place * uv_rows : (place + 1) * uv_rows]

    for flat in range(2 * rank // uv_rows, devices):
        block, level, core = flat // (stack * 2), flat // 2 % stack, flat % 2
        part_uv[block, level, core] = jnp.zeros((uv_rows, width), half)
    low_grad = contract_cols(slope_buf[...], cross_v_ref[...]).astype(half)
    low_turned = turned(low)
    grad_turned = turned(low_grad)
    for cols in tiles(width):
        keep_uv(0, cols, dot(grad_turned, input_ref[:, cols]).astype(half))
        keep_uv(rank, cols, dot(low_turned, slope_buf[:, cols]).astype(half))
    order = [turn(g, k, groups) for k in range(1, groups)] + [g]
    uv_pair = [send(part_uv.at[block, :, 1 - c], pair_uv.at[block], g, z, 1 - c) for block in order]

    for cols in tiles(width):
        value = (pool_buf[:, cols] + contract_cols(low_grad, cross_u_ref[cols, :])).astype(half)
        for place in range(value.shape[1] // row_width):
            feature = cols.start // row_width + place
            pair_buf[feature * samples : (feature + 1) * samples, :] = value[
                :, place * row_width : (place + 1) * row_width
            ]

    spots = (hot_slots, pairs)
    pick = lax.broadcasted_iota(jnp.int32, spots, 0) == hot_ref[...]
    pick = jnp.where(pick, 1.0, 0.0).astype(half)
    all_small[g, z, c, :hot_slots, :] = dot(pick, pair_buf[...]).astype(half)
    all_small[g, z, c, hot_slots:, :] = sums_buf[...].astype(half)
    own = all_small.at[g, z, c]
    small_z = [send(own, own, g, turn(z, k, stack), c) for k in range(1, stack)]

    uv_g = []
    for k, block in enumerate(order):
        landed(uv_pair[k : k + 1])

        @pl.loop(0, stack)
        def _(level, block=block):
            sum_uv[block, level] = (wide(part_uv[block, level, c]) + wide(pair_uv[block, level])).astype(half)

        if k < groups - 1:
            uv_g.append(send(sum_uv.at[block], in_uv.at[k], block, z, c))

    cells = (capacity, capacity)
    corner = lax.broadcasted_iota(jnp.int32, cells, 0) == lax.broadcasted_iota(jnp.int32, cells, 1)

    def rows_for(to):
        wish = source_ref[to].astype(jnp.float32)
        column = jnp.sum(jnp.where(corner, wish, 0.0), axis=1, keepdims=True).astype(jnp.int32)
        pick = lax.broadcasted_iota(jnp.int32, (capacity, pairs), 1) == column
        pick = jnp.where(pick, 1.0, 0.0).astype(half)
        return dot(pick, pair_buf[...]).astype(half)

    def give(first, last):
        @pl.loop(first, last)
        def _(k):
            to = turn(me, k, devices)
            grad_rows[to] = rows_for(to)
            hand(k).start()

    def add_rows_of(source):
        index = held_ref[source]
        grads = cold_in[source]
        step = 256
        for first in range(0, cold_out.shape[0], step):
            pick = lax.broadcasted_iota(jnp.int32, (step, capacity), 0) + first == index
            pick = jnp.where(pick, 1.0, 0.0).astype(half)
            cold_out[first : first + step, :] += dot(pick, grads)

    def take(first, last):
        @pl.loop(first, last)
        def _(k):
            hand(k).wait_recv()
            add_rows_of(turn(me, devices - k, devices))

    def part_of(eighths):
        return max(devices * eighths // 8, 1)

    give(1, part_of(8))

    landed(outs_sent)
    landed(turned_sent)
    former = jnp.concatenate([turned_all[block] for block in range(groups)], axis=1)
    for cols in tiles(width):
        latter = outs_all[:, :, cols].reshape(groups * samples, cols.stop - cols.start)
        part = dot(former, latter).astype(half)
        for level in range(stack):
            for core in range(2):
                first = (level * 2 + core) * rows
                part_mlp[level, core, :, cols] = part[first : first + rows]
    mlp_pair = [send(part_mlp.at[:, 1 - c], pair_mlp, g, z, 1 - c)]

    landed(uv_g)

    @pl.loop(0, stack)
    def _(level):
        value = wide(sum_uv[g, level])
        for k in range(groups - 1):
            value = value + wide(in_uv[k, level])
        zsum_uv[level] = value.astype(half)

    uv_z = []
    for k in range(1, stack):
        to_z = turn(z, k, stack)
        uv_z.append(send(zsum_uv.at[to_z], end_uv.at[k - 1], g, to_z, c))

    landed(mlp_pair)

    @pl.loop(0, stack)
    def _(level):
        sum_mlp[level] = (wide(part_mlp[level, c]) + wide(pair_mlp[level])).astype(half)

    mlp_z = []

    def send_mlp(first, last):
        for k in range(first, last):
            to_z = turn(z, k, stack)
            mlp_z.append(send(sum_mlp.at[to_z], end_mlp.at[k - 1], g, to_z, c))

    send_mlp(1, stack)
    landed(small_z)
    column = all_small.at[g, :, c]
    small_g = [send(column, column, turn(g, k, groups), z, c) for k in range(1, groups)]
    landed(uv_z)
    value = wide(zsum_uv[z])
    for k in range(stack - 1):
        value = value + wide(end_uv[k])
    all_uv[g, z, c] = value.astype(half)
    own = all_uv.at[g, z, c]
    all_z = [send(own, own, g, turn(z, k, stack), c) for k in range(1, stack)]
    cold_in[me] = rows_for(me)
    cold_out[...] = jnp.zeros_like(cold_out)
    add_rows_of(me)

    landed(all_z)
    column = all_uv.at[g, :, c]
    all_g = [send(column, column, turn(g, k, groups), z, c) for k in range(1, groups)]
    landed(small_g)
    parity = all_small.at[:, :, c]
    small_c = [send(parity, parity, g, z, 1 - c)]
    take(1, part_of(4))

    landed(all_g)
    parity = all_uv.at[:, :, c]
    all_c = [send(parity, parity, g, z, 1 - c)]
    landed(small_c)
    small_out[...] = all_small[...]
    take(part_of(4), devices)

    landed(mlp_z)
    value = wide(sum_mlp[z])
    for k in range(stack - 1):
        value = value + wide(end_mlp[k])
    mlp_out[...] = value

    landed(all_c)
    for flat in range(2 * rank // uv_rows):
        block, level, core = flat // (stack * 2), flat // 2 % stack, flat % 2
        uv_out[flat * uv_rows : (flat + 1) * uv_rows, :] = all_uv[block, level, core]

    for copy in started:
        copy.wait_send()

    @pl.loop(1, devices)
    def _(k):
        hand(k).wait_send()


def train(first_input, cross_u, cross_v, cross_bias, mlp_weight, mlp_bias, out_weight, labels, source, held, hot, lists, hot_slots, shard_rows):
    groups = lax.axis_size("grp")
    stack = lax.axis_size("dev") // 2
    devices = groups * stack * 2
    samples, width = first_input.shape
    rank = cross_v.shape[0]
    hidden_width = mlp_weight.shape[0]
    rows = hidden_width // devices
    uv_rows = -(-2 * rank // (16 * devices)) * 16
    capacity = source.shape[-1]
    row_width = lists.shape[1]
    pairs = hot.shape[1]
    half, full = jnp.bfloat16, jnp.float32
    sum_rows = 2 + (width + 2 * hidden_width) // row_width
    sum_rows = -(-sum_rows // 16) * 16
    small_rows = hot_slots + sum_rows
    share = hidden_width // groups
    lead = (groups, stack, 2)
    scratch = [
        ((samples, width), full),
        ((samples, hidden_width), full),
        ((samples, hidden_width), full),
        ((samples, hidden_width), half),
        ((samples, hidden_width), half),
        ((groups, share, samples), half),
        ((samples, width), full),
        ((samples, width), half),
        ((pairs, row_width), half),
        ((sum_rows, row_width), full),
        ((stack, 2, rows, width), half),
        (lead + (uv_rows, width), half),
        ((devices, capacity, row_width), half),
        ((groups, samples, width), half),
        ((groups, share, samples), half),
        ((stack, rows, width), half),
        ((stack, rows, width), half),
        ((stack - 1, rows, width), half),
        ((groups, stack, uv_rows, width), half),
        ((groups, stack, uv_rows, width), half),
        ((groups - 1, stack, uv_rows, width), half),
        ((stack, uv_rows, width), half),
        ((stack - 1, uv_rows, width), half),
        (lead + (uv_rows, width), half),
        (lead + (small_rows, row_width), half),
        ((devices, capacity, row_width), half),
    ]
    outs = [
        ((rows, width), full),
        ((2 * rank, width), half),
        (lead + (small_rows, row_width), half),
        ((shard_rows, row_width), full),
    ]
    copies = 5 * (groups - 1) + 3 + groups + 4 * (stack - 1) + 3
    whole = pl.BlockSpec(memory_space=pltpu.VMEM)
    args = (first_input, cross_u, cross_v, cross_bias, mlp_weight, mlp_bias, out_weight, labels, source, held, hot, lists)
    size = sum(math.prod(shape) * jnp.dtype(kind).itemsize for shape, kind in scratch + outs)
    size += sum(arg.size * arg.dtype.itemsize for arg in args) + devices * capacity * 64
    limit = min(size + 6 * 1024 * 1024, 61 * 1024 * 1024)
    return pl.pallas_call(
        functools.partial(train_kernel, groups, stack),
        in_specs=[whole] * len(args),
        out_specs=[whole] * 4,
        out_shape=[jax.ShapeDtypeStruct(shape, kind) for shape, kind in outs],
        scratch_shapes=[pltpu.VMEM(shape, kind) for shape, kind in scratch]
        + [pltpu.SemaphoreType.DMA((copies,))] * 2
        + [pltpu.SemaphoreType.DMA((devices,))] * 2,
        compiler_params=pltpu.CompilerParams(collective_id=0, has_side_effects=True, vmem_limit_bytes=limit),
    )(*args)


def fetch_kernel(
    devices,
    slot_ref,
    place_ref,
    base_ref,
    table_ref,
    out_ref,
    asked_ref,
    asked,
    found,
    arrived,
    total,
    ask_send,
    ask_recv,
    row_send,
    row_recv,
):
    per_group = lax.axis_size("dev")
    me = lax.axis_index("grp") * per_group + lax.axis_index("dev")
    mesh_id = pl.DeviceIdType.MESH
    capacity = slot_ref.shape[-1]
    shard_rows, row_width = table_ref.shape
    pairs, bags = place_ref.shape
    samples = out_ref.shape[0]

    def spot(flat):
        return (lax.div(flat, per_group), lax.rem(flat, per_group))

    def after(k):
        return lax.rem(me + k, devices)

    def before(k):
        return lax.rem(me + devices - k, devices)

    def ask(k):
        return pltpu.make_async_remote_copy(
            src_ref=slot_ref.at[after(k)],
            dst_ref=asked.at[me],
            send_sem=ask_send.at[k],
            recv_sem=ask_recv.at[k],
            device_id=spot(after(k)),
            device_id_type=mesh_id,
        )

    def answer(k):
        return pltpu.make_async_remote_copy(
            src_ref=found.at[before(k)],
            dst_ref=arrived.at[me],
            send_sem=row_send.at[k],
            recv_sem=row_recv.at[k],
            device_id=spot(before(k)),
            device_id_type=mesh_id,
        )

    barrier = pltpu.get_barrier_semaphore()

    @pl.loop(1, devices)
    def _(k):
        pl.semaphore_signal(barrier, inc=1, device_id=spot(after(k)), device_id_type=mesh_id)

    pl.semaphore_wait(barrier, devices - 1)

    @pl.loop(1, devices)
    def _(k):
        ask(k).start()

    asked[me] = slot_ref[me]
    total[...] = base_ref[...]

    square = (capacity, capacity)
    diagonal = lax.broadcasted_iota(jnp.int32, square, 0) == lax.broadcasted_iota(jnp.int32, square, 1)

    def rows_for(owner_of):
        wish = asked[owner_of].astype(jnp.float32)
        column = jnp.sum(jnp.where(diagonal, wish, 0.0), axis=1, keepdims=True).astype(jnp.int32) - 1
        value = jnp.zeros((capacity, row_width), jnp.float32)
        step = 512
        for first in range(0, shard_rows, step):
            pick = lax.broadcasted_iota(jnp.int32, (capacity, step), 1) + first == column
            pick = jnp.where(pick, 1.0, 0.0).astype(jnp.bfloat16)
            value = value + jnp.dot(
                pick, table_ref[first : first + step, :], preferred_element_type=jnp.float32
            )
        return value.astype(jnp.bfloat16)

    @pl.loop(1, devices)
    def _(k):
        ask(k).wait_recv()
        found[before(k)] = rows_for(before(k))
        answer(k).start()

    arrived[me] = rows_for(me)

    chunk = pairs // 4

    def gather_in(source):
        rows = arrived[source]
        for first in range(0, pairs, chunk):
            places = place_ref[first : first + chunk, :] - source * capacity
            lane = lax.broadcasted_iota(jnp.int32, (chunk, capacity), 1)
            hit = lane == places[:, 0:1]
            for bag in range(1, bags):
                hit = hit | (lane == places[:, bag : bag + 1])
            hit = jnp.where(hit, 1.0, 0.0).astype(jnp.bfloat16)
            total[first : first + chunk, :] += jnp.dot(hit, rows, preferred_element_type=jnp.float32)

    gather_in(me)

    @pl.loop(1, devices)
    def _(k):
        answer(k).wait_recv()
        gather_in(after(k))

    for feature in range(pairs // samples):
        out_ref[:, feature * row_width : (feature + 1) * row_width] = total[
            feature * samples : (feature + 1) * samples, :
        ].astype(out_ref.dtype)
    asked_ref[...] = asked[...]

    @pl.loop(1, devices)
    def _(k):
        ask(k).wait_send()
        answer(k).wait_send()


def fetch(slots, places, base, table, samples):
    devices, capacity = slots.shape
    pairs, row_width = base.shape
    whole = pl.BlockSpec(memory_space=pltpu.VMEM)
    block = (devices, capacity, row_width)
    first_input, asked = pl.pallas_call(
        functools.partial(fetch_kernel, devices),
        in_specs=[whole] * 4,
        out_specs=[whole] * 2,
        out_shape=[
            jax.ShapeDtypeStruct((samples, pairs // samples * row_width), jnp.bfloat16),
            jax.ShapeDtypeStruct((devices, 1, capacity), jnp.int32),
        ],
        scratch_shapes=[
            pltpu.VMEM((devices, 1, capacity), jnp.int32),
            pltpu.VMEM(block, jnp.bfloat16),
            pltpu.VMEM(block, jnp.bfloat16),
            pltpu.VMEM((pairs, row_width), jnp.float32),
        ]
        + [pltpu.SemaphoreType.DMA((devices,))] * 4,
        compiler_params=pltpu.CompilerParams(
            collective_id=1, has_side_effects=True, vmem_limit_bytes=32 * 1024 * 1024
        ),
    )(slots.reshape(devices, 1, capacity), places, base, table)
    return first_input, asked.reshape(devices, capacity)


def contract_rows(former, latter):
    return lax.dot_general(
        former, latter, (((0,), (0,)), ((), ())), preferred_element_type=jnp.float32
    )


def contract_cols(former, latter):
    return lax.dot_general(
        former, latter, (((1,), (1,)), ((), ())), preferred_element_type=jnp.float32
    )


def per_device(
    ids,
    location,
    cold_table,
    hot_index,
    hot_list,
    hot_table,
    labels,
    cross_u,
    cross_v,
    cross_bias,
    mlp_weight,
    mlp_bias,
    out_weight,
):
    devices = lax.axis_size(BOTH)
    samples, features, bag_size = ids.shape
    shard_rows, row_width = cold_table.shape
    pairs = samples * features
    requests = pairs * bag_size
    mean_load = requests // devices
    capacity = -(-(mean_load + mean_load // 2) // 16) * 16
    placed = look_up(location, ids.transpose(2, 1, 0).reshape(requests))
    owners = placed // shard_rows
    row_slot = placed - owners * shard_rows
    by_owner = owners[:, None] == jnp.arange(devices, dtype=jnp.int32)[None, :]
    member = by_owner.astype(jnp.bfloat16)
    counted = rank_among(member, samples)
    rank = jnp.sum(jnp.where(by_owner, counted, 0.0), axis=1).astype(jnp.int32)
    position = owners * capacity + rank
    ranked = rank[:, None] == jnp.arange(capacity, dtype=jnp.int32)[None, :]
    pair = jnp.arange(requests, dtype=jnp.int32) % pairs
    tables = digits_of(row_slot + 1, shard_rows + 1)
    cut = len(tables)
    tables = tables + digits_of(pair, pairs)
    sheet = jnp.concatenate(
        [jnp.where(ranked, part.astype(jnp.float32)[:, None], 0.0) for part in tables], axis=1
    ).astype(jnp.bfloat16)
    laid = contract_rows(member, sheet).astype(jnp.int32)

    def joined(first, last):
        total = 0
        for place in range(first, last):
            total = total + laid[:, place * capacity : (place + 1) * capacity] * (256 ** (place - first))
        return total

    send_slot = joined(0, cut)
    source = joined(cut, len(tables)).reshape(devices * capacity)
    hot_slots = hot_list.shape[1]
    hot_flat = hot_index.transpose(1, 0).reshape(pairs)
    selector = (hot_flat[:, None] == jnp.arange(hot_slots, dtype=jnp.int32)[None, :]).astype(jnp.bfloat16)
    pooled = jnp.dot(selector, hot_table[hot_list[0]], preferred_element_type=jnp.float32)
    places = position.reshape(bag_size, pairs).transpose(1, 0)
    first_input, wanted = fetch(send_slot, places, pooled, cold_table, samples)
    held = (wanted - 1).reshape(devices, 1, capacity)
    lane_pad = (0, -hot_slots % row_width)
    lists = jnp.stack([jnp.pad(digit, lane_pad) for digit in (hot_list[0] // 64, hot_list[0] % 64)])
    mlp_weight_grad, uv_sum, every_small, cold_grad = train(
        first_input,
        cross_u,
        cross_v,
        cross_bias[None, :],
        mlp_weight,
        mlp_bias[None, :],
        out_weight.astype(jnp.float32)[None, :],
        labels[None, :],
        source.reshape(devices, 1, capacity),
        held,
        hot_flat[None, :],
        lists.astype(jnp.float32),
        hot_slots,
        shard_rows,
    )
    rank_width, in_width = cross_v.shape
    hidden_width = mlp_bias.shape[0]
    every_small = every_small.reshape(devices, -1, row_width)
    every_block = every_small[:, :hot_slots].reshape(devices * hot_slots, row_width)
    every_list = every_small[:, hot_slots : hot_slots + 2, :hot_slots].astype(jnp.int32)
    every_row = (every_list[:, 0] * 64 + every_list[:, 1]).reshape(devices * hot_slots)
    hot_grad = add_rows(every_row, every_block, hot_table.shape[0])
    added = jnp.sum(every_small[:, hot_slots + 2 :].astype(jnp.float32), axis=0).reshape(-1)
    cross_u_grad = uv_sum[:rank_width].transpose(1, 0).astype(jnp.float32)
    cross_v_grad = uv_sum[rank_width : 2 * rank_width].astype(jnp.float32)
    cross_bias_grad = added[:in_width]
    mlp_bias_grad = added[in_width : in_width + hidden_width]
    out_weight_grad = added[in_width + hidden_width : in_width + 2 * hidden_width]
    return (
        cold_grad,
        hot_grad,
        mlp_weight_grad,
        cross_u_grad,
        cross_v_grad,
        cross_bias_grad,
        mlp_bias_grad,
        out_weight_grad,
    )


def solution(mesh):
    placed = (
        P(("grp", "dev"), None, None),
        P(),
        P(("grp", "dev"), None),
        P(("grp", "dev"), None),
        P(("grp", "dev"), None),
        P(),
        P(("grp", "dev")),
        P(),
        P(),
        P(),
        P(),
        P(),
        P(),
    )
    return jax.shard_map(
        per_device,
        mesh=mesh,
        in_specs=placed,
        out_specs=(P(("grp", "dev"), None), P(), P(("grp", "dev"), None), P(), P(), P(), P(), P()),
        check_vma=False,
    )
```

```python
import functools
import math

import jax
import jax.numpy as jnp
from jax import lax
from jax.experimental import pallas as pl
from jax.experimental.pallas import tpu as pltpu
from jax.sharding import PartitionSpec as P

BOTH = ("grp", "dev")


def digits_of(values, limit):
    parts = []
    while limit > 1:
        parts.append(values % 256)
        values = values // 256
        limit = -(-limit // 256)
    return parts


def look_up(table, index):
    size = table.shape[0]
    lanes = 128
    rows = size // lanes
    parts = digits_of(table.reshape(rows, lanes), size)
    stacked = jnp.concatenate(parts, axis=1).astype(jnp.bfloat16)
    pick = (index[:, None] // lanes == jnp.arange(rows, dtype=jnp.int32)[None, :]).astype(jnp.bfloat16)
    found = jnp.dot(pick, stacked, preferred_element_type=jnp.float32)
    lane = (index[:, None] % lanes) == jnp.arange(lanes, dtype=jnp.int32)[None, :]
    total = 0.0
    for place in range(len(parts)):
        total = total + found[:, place * lanes : (place + 1) * lanes] * float(256**place)
    return jnp.sum(jnp.where(lane, total, 0.0), axis=1).astype(jnp.int32)


def rank_among(member, block):
    count, width = member.shape
    pieces = member.reshape(count // block, block, width)
    below = jnp.tril(jnp.ones((block, block), jnp.bfloat16), -1)
    inner = jnp.einsum("ij,bjd->bid", below, pieces, preferred_element_type=jnp.float32)
    sums = jnp.sum(pieces.astype(jnp.float32), axis=1)
    over = jnp.tril(jnp.ones((count // block, count // block), jnp.bfloat16), -1)
    outer = jnp.dot(over, sums.astype(jnp.bfloat16), preferred_element_type=jnp.float32)
    return (inner + outer[:, None, :]).reshape(count, width)


def tiles(width, step=256):
    return [slice(first, min(first + step, width)) for first in range(0, width, step)]


def train_kernel(
    groups,
    stack,
    input_ref,
    cross_u_ref,
    cross_v_ref,
    cross_bias_ref,
    mlp_hbm,
    mlp_bias_ref,
    out_weight_ref,
    label_ref,
    source_ref,
    held_ref,
    hot_ref,
    list_ref,
    mlp_out,
    cross_u_out,
    cross_v_out,
    hidden_bias_out,
    out_weight_out,
    cross_bias_out,
    hot_out,
    cold_out,
    mlp_ref,
    flat_uv,
    term_buf,
    hidden_buf,
    squash_buf,
    active_buf,
    grad_buf,
    turned_buf,
    pool_buf,
    slope_buf,
    pair_buf,
    sums_buf,
    part_mlp,
    part_uv,
    grad_rows,
    outs_all,
    turned_all,
    pair_mlp,
    sum_mlp,
    end_mlp,
    pair_uv,
    sum_uv,
    in_uv,
    zsum_uv,
    end_uv,
    all_uv,
    all_small,
    cold_in,
    send_sem,
    recv_sem,
    row_send,
    row_recv,
    load_sem,
):
    g = lax.axis_index("grp")
    d = lax.axis_index("dev")
    z = lax.div(d, 2)
    c = lax.rem(d, 2)
    half = jnp.bfloat16
    mesh_id = pl.DeviceIdType.MESH
    samples, width = input_ref.shape
    rank = cross_v_ref.shape[0]
    hidden_width = mlp_ref.shape[0]
    rows = mlp_out.shape[0]
    uv_rows = part_uv.shape[3]
    capacity = source_ref.shape[-1]
    pairs, row_width = pair_buf.shape
    hot_slots = all_small.shape[3] - sums_buf.shape[0]
    devices = groups * stack * 2
    me = g * (stack * 2) + d

    def turn(here, by, size):
        return lax.rem(here + by, size)

    def spot(flat):
        return (lax.div(flat, stack * 2), lax.rem(flat, stack * 2))

    def wide(value):
        return value.astype(jnp.float32)

    def dot(former, latter):
        return jnp.dot(former, latter, preferred_element_type=jnp.float32)

    def turned(value):
        return wide(value).T.astype(half)

    started = []

    def send(source, target, to_g, to_z, to_c):
        place = len(started)
        copy = pltpu.make_async_remote_copy(
            src_ref=source,
            dst_ref=target,
            send_sem=send_sem.at[place],
            recv_sem=recv_sem.at[place],
            device_id=(to_g, to_z * 2 + to_c),
            device_id_type=mesh_id,
        )
        copy.start()
        started.append(copy)
        return copy

    def landed(copies):
        for copy in copies:
            copy.wait_recv()

    def own_rows(flat):
        return pl.ds(pl.multiple_of(flat * capacity, 16), capacity)

    def hand(k):
        to = turn(me, k, devices)
        return pltpu.make_async_remote_copy(
            src_ref=grad_rows.at[to],
            dst_ref=cold_in.at[me],
            send_sem=row_send.at[k],
            recv_sem=row_recv.at[k],
            device_id=spot(to),
            device_id_type=mesh_id,
        )

    barrier = pltpu.get_barrier_semaphore()

    @pl.loop(1, devices)
    def _(k):
        pl.semaphore_signal(barrier, inc=1, device_id=spot(turn(me, k, devices)), device_id_type=mesh_id)

    loads = []
    for place, cols in enumerate(tiles(hidden_width)):
        loads.append(pltpu.make_async_copy(mlp_hbm.at[cols], mlp_ref.at[cols], load_sem.at[place]))
        loads[-1].start()

    low = dot(input_ref[...], cross_u_ref[...]).astype(half)
    for cols in tiles(width):
        term = dot(low, cross_v_ref[:, cols]) + cross_bias_ref[:, cols]
        value = wide(input_ref[:, cols])
        term_buf[:, cols] = term
        outs_all[g, :, cols] = (value * term + value).astype(half)

    pl.semaphore_wait(barrier, devices - 1)
    paired = groups == 4
    across = lax.div(g, 2) * 2 + 1 - lax.rem(g, 2)
    along = turn(g, 2, groups)
    middle = (width // row_width + 1) // 2 * row_width
    left, right = slice(0, middle), slice(middle, width)

    def send_outs(block, cols, to_g):
        piece = outs_all.at[block, :, cols]
        return send(piece, piece, to_g, z, c)

    if paired:
        outs_first = [send_outs(g, left, across), send_outs(g, right, along)]
        outs_sent = [send_outs(g, right, across), send_outs(g, left, along)]
    else:
        outs_sent = [send_outs(g, slice(0, width), turn(g, k, groups)) for k in range(1, groups)]

    score = jnp.zeros((samples, 1), jnp.float32)
    for load, cols in zip(loads, tiles(hidden_width)):
        load.wait()
        value = contract_cols(outs_all[g], mlp_ref[cols, :]) + mlp_bias_ref[:, cols]
        squash = jax.nn.sigmoid(value)
        active = (value * squash).astype(half)
        hidden_buf[:, cols] = value
        squash_buf[:, cols] = squash
        active_buf[:, cols] = active
        score = score + jnp.sum(wide(active) * out_weight_ref[:, cols], axis=1, keepdims=True)

    square = (samples, samples)
    diagonal = lax.broadcasted_iota(jnp.int32, square, 0) == lax.broadcasted_iota(jnp.int32, square, 1)
    label = jnp.sum(jnp.where(diagonal, wide(label_ref[...]), 0.0), axis=1, keepdims=True)
    score_grad = jax.nn.sigmoid(score) - label

    sums_buf[...] = jnp.zeros_like(sums_buf)

    def keep_sum(first, cols, value):
        start = first + cols.start // row_width
        for place in range(value.shape[1] // row_width):
            sums_buf[start + place : start + place + 1, :] = value[:, place * row_width : (place + 1) * row_width]

    hidden_rows, width_rows = hidden_width // row_width, width // row_width
    bias_at, out_at, cross_at = 0, hidden_rows, 2 * hidden_rows
    list_at = cross_at + width_rows
    sums_buf[list_at : list_at + 2, :] = list_ref[...]
    share = hidden_width // groups
    for cols in tiles(hidden_width):
        value = hidden_buf[:, cols]
        squash = squash_buf[:, cols]
        slope = squash * (1.0 + value * (1.0 - squash))
        grad = (score_grad * out_weight_ref[:, cols] * slope).astype(half)
        grad_buf[:, cols] = grad
        keep_sum(bias_at, cols, jnp.sum(wide(grad), axis=0, keepdims=True))
        keep_sum(out_at, cols, jnp.sum(wide(active_buf[:, cols]) * score_grad, axis=0, keepdims=True))
        inside = cols.start % share
        turned_buf[cols.start // share, inside : inside + cols.stop - cols.start, :] = turned(grad)
    turned_all[g] = turned_buf[g]

    for cols in tiles(width):
        back = dot(grad_buf[...], mlp_ref[:, cols])
        slope = (back * wide(input_ref[:, cols])).astype(half)
        slope_buf[:, cols] = slope
        pool_buf[:, cols] = back * (term_buf[:, cols] + 1.0)
        keep_sum(cross_at, cols, jnp.sum(wide(slope), axis=0, keepdims=True))

    def keep_uv(first, cols, part):
        for place in range(rank // uv_rows):
            flat = first // uv_rows + place
            block, level, core = flat // (stack * 2), flat // 2 % stack, flat % 2
            part_uv[block, level, core, :, cols] = part[place * uv_rows : (place + 1) * uv_rows]

    for flat in range(2 * rank // uv_rows, devices):
        block, level, core = flat // (stack * 2), flat // 2 % stack, flat % 2
        part_uv[block, level, core] = jnp.zeros((uv_rows, width), half)
    low_grad = contract_cols(slope_buf[...], cross_v_ref[...]).astype(half)
    low_turned = turned(low)
    grad_turned = turned(low_grad)
    for cols in tiles(width):
        keep_uv(0, cols, dot(grad_turned, input_ref[:, cols]).astype(half))
        keep_uv(rank, cols, dot(low_turned, slope_buf[:, cols]).astype(half))
    order = [turn(g, k, groups) for k in range(1, groups)] + [g]
    uv_pair = [send(part_uv.at[block, :, 1 - c], pair_uv.at[block], g, z, 1 - c) for block in order]

    for cols in tiles(width):
        value = (pool_buf[:, cols] + contract_cols(low_grad, cross_u_ref[cols, :])).astype(half)
        for place in range(value.shape[1] // row_width):
            feature = cols.start // row_width + place
            pair_buf[feature * samples : (feature + 1) * samples, :] = value[
                :, place * row_width : (place + 1) * row_width
            ]

    spots = (hot_slots, pairs)
    pick = lax.broadcasted_iota(jnp.int32, spots, 0) == hot_ref[...]
    pick = jnp.where(pick, 1.0, 0.0).astype(half)
    all_small[g, z, c, :hot_slots, :] = dot(pick, pair_buf[...]).astype(half)
    all_small[g, z, c, hot_slots:, :] = sums_buf[...].astype(half)
    own = all_small.at[g, z, c]
    small_z = [send(own, own, g, turn(z, k, stack), c) for k in range(1, stack)]

    uv_g = []
    for k, block in enumerate(order):
        landed(uv_pair[k : k + 1])

        @pl.loop(0, stack)
        def _(level, block=block):
            sum_uv[block, level] = (wide(part_uv[block, level, c]) + wide(pair_uv[block, level])).astype(half)

        if k < groups - 1:
            uv_g.append(send(sum_uv.at[block], in_uv.at[k], block, z, c))

    cells = (capacity, capacity)
    corner = lax.broadcasted_iota(jnp.int32, cells, 0) == lax.broadcasted_iota(jnp.int32, cells, 1)

    def rows_for(to):
        wish = source_ref[to].astype(jnp.float32)
        column = jnp.sum(jnp.where(corner, wish, 0.0), axis=1, keepdims=True).astype(jnp.int32)
        pick = lax.broadcasted_iota(jnp.int32, (capacity, pairs), 1) == column
        pick = jnp.where(pick, 1.0, 0.0).astype(half)
        return dot(pick, pair_buf[...]).astype(half)

    def give(first, last):
        @pl.loop(first, last)
        def _(k):
            to = turn(me, k, devices)
            grad_rows[to] = rows_for(to)
            hand(k).start()

    def add_rows_of(source):
        index = held_ref[source]
        grads = cold_in[source]
        step = 256
        for first in range(0, cold_out.shape[0], step):
            pick = lax.broadcasted_iota(jnp.int32, (step, capacity), 0) + first == index
            pick = jnp.where(pick, 1.0, 0.0).astype(half)
            cold_out[first : first + step, :] += dot(pick, grads)

    def take(first, last):
        @pl.loop(first, last)
        def _(k):
            hand(k).wait_recv()
            add_rows_of(turn(me, devices - k, devices))

    def part_of(eighths):
        return max(devices * eighths // 8, 1)

    if paired:
        landed(outs_first)
        outs_sent += [send_outs(across, left, along), send_outs(along, right, across)]
    turned_sent = []
    for k in range(1, groups):
        to_g = turn(g, k, groups)
        turned_sent.append(send(turned_buf.at[to_g], turned_all.at[g], to_g, z, c))
    give(1, part_of(3))

    landed(uv_g)

    @pl.loop(0, stack)
    def _(level):
        value = wide(sum_uv[g, level])
        for k in range(groups - 1):
            value = value + wide(in_uv[k, level])
        zsum_uv[level] = value.astype(half)

    uv_z = []
    for k in range(1, stack):
        to_z = turn(z, k, stack)
        uv_z.append(send(zsum_uv.at[to_z], end_uv.at[k - 1], g, to_z, c))

    give(part_of(3), part_of(5))

    landed(uv_z)
    value = wide(zsum_uv[z])
    for k in range(stack - 1):
        value = value + wide(end_uv[k])
    all_uv[g, z, c] = value.astype(half)
    own = all_uv.at[g, z, c]
    all_z = [send(own, own, g, turn(z, k, stack), c) for k in range(1, stack)]
    landed(outs_sent)
    landed(turned_sent)
    former = jnp.concatenate([turned_all[block] for block in range(groups)], axis=1)
    for cols in tiles(width):
        latter = outs_all[:, :, cols].reshape(groups * samples, cols.stop - cols.start)
        part = dot(former, latter).astype(half)
        for level in range(stack):
            for core in range(2):
                first = (level * 2 + core) * rows
                part_mlp[level, core, :, cols] = part[first : first + rows]
    mlp_pair = [send(part_mlp.at[:, 1 - c], pair_mlp, g, z, 1 - c)]

    give(part_of(5), devices)

    landed(mlp_pair)

    @pl.loop(0, stack)
    def _(level):
        sum_mlp[level] = (wide(part_mlp[level, c]) + wide(pair_mlp[level])).astype(half)

    mlp_z = []

    def send_mlp(first, last):
        for k in range(first, last):
            to_z = turn(z, k, stack)
            mlp_z.append(send(sum_mlp.at[to_z], end_mlp.at[k - 1], g, to_z, c))

    send_mlp(1, stack)
    landed(small_z)
    column = all_small.at[g, :, c]
    small_g = [send(column, column, turn(g, k, groups), z, c) for k in range(1, groups)]
    cold_in[me] = rows_for(me)
    cold_out[...] = jnp.zeros_like(cold_out)
    add_rows_of(me)

    landed(all_z)
    column = all_uv.at[g, :, c]
    all_g = [send(column, column, turn(g, k, groups), z, c) for k in range(1, groups)]
    landed(small_g)
    parity = all_small.at[:, :, c]
    small_c = [send(parity, parity, g, z, 1 - c)]
    take(1, part_of(4))

    landed(all_g)
    parity = all_uv.at[:, :, c]
    all_c = [send(parity, parity, g, z, 1 - c)]
    landed(small_c)

    @pl.loop(0, groups, init_carry=jnp.zeros(sums_buf.shape, jnp.float32))
    def added(block, total):
        for level in range(stack):
            for core in range(2):
                total = total + wide(all_small[block, level, core, hot_slots:, :])
        return total

    hidden_bias_out[...] = added[bias_at:out_at]
    out_weight_out[...] = added[out_at:cross_at]
    cross_bias_out[...] = added[cross_at:list_at]
    hot_out[...] = jnp.zeros_like(hot_out)
    quad = row_width // hot_slots

    def listed(block, level):
        total = jnp.zeros(sums_buf.shape, jnp.float32)
        for place in range(quad):
            total = total + wide(all_small[block, level + place // 2, place % 2, hot_slots:, :])
        row = total[list_at : list_at + 1] * 64.0 + total[list_at + 1 : list_at + 2]
        return row.astype(jnp.int32)

    @pl.loop(0, groups)
    def _(block):
        @pl.loop(0, stack // quad)
        def _(part):
            level = part * quad
            levels = [level, level + quad // 2]
            index = jnp.concatenate([listed(block, first) for first in levels], axis=1)
            grads = all_small[block, pl.ds(level, quad), :, :hot_slots, :]
            grads = grads.reshape(2 * quad * hot_slots, row_width)
            step = 512
            for first in range(0, hot_out.shape[0], step):
                pick = lax.broadcasted_iota(jnp.int32, (step, 2 * row_width), 0) + first == index
                pick = jnp.where(pick, 1.0, 0.0).astype(half)
                hot_out[first : first + step, :] += dot(pick, grads)

    take(part_of(4), devices)

    landed(mlp_z)
    value = wide(sum_mlp[z])
    for k in range(stack - 1):
        value = value + wide(end_mlp[k])
    mlp_out[...] = value

    landed(all_c)
    for flat in range(2 * rank // uv_rows):
        block, level, core = flat // (stack * 2), flat // 2 % stack, flat % 2
        first = flat * uv_rows
        if first < rank:
            flat_uv[first : first + uv_rows, :] = wide(all_uv[block, level, core])
        else:
            cross_v_out[first - rank : first - rank + uv_rows, :] = wide(all_uv[block, level, core])
    for cols in tiles(width):
        cross_u_out[cols, :] = flat_uv[:, cols].T

    for copy in started:
        copy.wait_send()

    @pl.loop(1, devices)
    def _(k):
        hand(k).wait_send()


def train(first_input, cross_u, cross_v, cross_bias, mlp_weight, mlp_bias, out_weight, labels, source, held, hot, lists, hot_slots, hot_rows, shard_rows):
    groups = lax.axis_size("grp")
    stack = lax.axis_size("dev") // 2
    devices = groups * stack * 2
    samples, width = first_input.shape
    rank = cross_v.shape[0]
    hidden_width = mlp_weight.shape[0]
    rows = hidden_width // devices
    uv_rows = -(-2 * rank // (16 * devices)) * 16
    capacity = source.shape[-1]
    row_width = lists.shape[1]
    pairs = hot.shape[1]
    half, full = jnp.bfloat16, jnp.float32
    sum_rows = 2 + (width + 2 * hidden_width) // row_width
    sum_rows = -(-sum_rows // 16) * 16
    small_rows = hot_slots + sum_rows
    share = hidden_width // groups
    lead = (groups, stack, 2)
    scratch = [
        ((hidden_width, width), half),
        ((rank, width), full),
        ((samples, width), full),
        ((samples, hidden_width), full),
        ((samples, hidden_width), full),
        ((samples, hidden_width), half),
        ((samples, hidden_width), half),
        ((groups, share, samples), half),
        ((samples, width), full),
        ((samples, width), half),
        ((pairs, row_width), half),
        ((sum_rows, row_width), full),
        ((stack, 2, rows, width), half),
        (lead + (uv_rows, width), half),
        ((devices, capacity, row_width), half),
        ((groups, samples, width), half),
        ((groups, share, samples), half),
        ((stack, rows, width), half),
        ((stack, rows, width), half),
        ((stack - 1, rows, width), half),
        ((groups, stack, uv_rows, width), half),
        ((groups, stack, uv_rows, width), half),
        ((groups - 1, stack, uv_rows, width), half),
        ((stack, uv_rows, width), half),
        ((stack - 1, uv_rows, width), half),
        (lead + (uv_rows, width), half),
        (lead + (small_rows, row_width), half),
        ((devices, capacity, row_width), half),
    ]
    outs = [
        ((rows, width), full),
        ((width, rank), full),
        ((rank, width), full),
        ((hidden_width // row_width, row_width), full),
        ((hidden_width // row_width, row_width), full),
        ((width // row_width, row_width), full),
        ((hot_rows, row_width), full),
        ((shard_rows, row_width), full),
    ]
    copies = 5 * (groups - 1) + 3 + groups + 4 * (stack - 1) + 3
    whole = pl.BlockSpec(memory_space=pltpu.VMEM)
    args = (first_input, cross_u, cross_v, cross_bias, mlp_weight, mlp_bias, out_weight, labels, source, held, hot, lists)
    size = sum(math.prod(shape) * jnp.dtype(kind).itemsize for shape, kind in scratch + outs)
    size += sum(arg.size * arg.dtype.itemsize for arg in args) - mlp_weight.size * 2 + devices * capacity * 64
    limit = min(size + 6 * 1024 * 1024, 61 * 1024 * 1024)
    return pl.pallas_call(
        functools.partial(train_kernel, groups, stack),
        in_specs=[whole] * 4 + [pl.BlockSpec(memory_space=pl.ANY)] + [whole] * (len(args) - 5),
        out_specs=[whole] * len(outs),
        out_shape=[jax.ShapeDtypeStruct(shape, kind) for shape, kind in outs],
        scratch_shapes=[pltpu.VMEM(shape, kind) for shape, kind in scratch]
        + [pltpu.SemaphoreType.DMA((copies,))] * 2
        + [pltpu.SemaphoreType.DMA((devices,))] * 2
        + [pltpu.SemaphoreType.DMA((len(tiles(hidden_width)),))],
        compiler_params=pltpu.CompilerParams(collective_id=0, has_side_effects=True, vmem_limit_bytes=limit),
    )(*args)


def fetch_kernel(
    devices,
    slot_ref,
    place_ref,
    base_ref,
    table_ref,
    out_ref,
    asked_ref,
    asked,
    found,
    arrived,
    total,
    ask_send,
    ask_recv,
    row_send,
    row_recv,
):
    per_group = lax.axis_size("dev")
    me = lax.axis_index("grp") * per_group + lax.axis_index("dev")
    mesh_id = pl.DeviceIdType.MESH
    capacity = slot_ref.shape[-1]
    shard_rows, row_width = table_ref.shape
    pairs, bags = place_ref.shape
    samples = out_ref.shape[0]

    def spot(flat):
        return (lax.div(flat, per_group), lax.rem(flat, per_group))

    def after(k):
        return lax.rem(me + k, devices)

    def before(k):
        return lax.rem(me + devices - k, devices)

    def ask(k):
        return pltpu.make_async_remote_copy(
            src_ref=slot_ref.at[after(k)],
            dst_ref=asked.at[me],
            send_sem=ask_send.at[k],
            recv_sem=ask_recv.at[k],
            device_id=spot(after(k)),
            device_id_type=mesh_id,
        )

    def answer(k):
        return pltpu.make_async_remote_copy(
            src_ref=found.at[before(k)],
            dst_ref=arrived.at[me],
            send_sem=row_send.at[k],
            recv_sem=row_recv.at[k],
            device_id=spot(before(k)),
            device_id_type=mesh_id,
        )

    barrier = pltpu.get_barrier_semaphore()

    @pl.loop(1, devices)
    def _(k):
        pl.semaphore_signal(barrier, inc=1, device_id=spot(after(k)), device_id_type=mesh_id)

    pl.semaphore_wait(barrier, devices - 1)

    @pl.loop(1, devices)
    def _(k):
        ask(k).start()

    asked[me] = slot_ref[me]
    total[...] = base_ref[...]

    square = (capacity, capacity)
    diagonal = lax.broadcasted_iota(jnp.int32, square, 0) == lax.broadcasted_iota(jnp.int32, square, 1)

    def rows_for(owner_of):
        wish = asked[owner_of].astype(jnp.float32)
        column = jnp.sum(jnp.where(diagonal, wish, 0.0), axis=1, keepdims=True).astype(jnp.int32) - 1
        value = jnp.zeros((capacity, row_width), jnp.float32)
        step = 512
        for first in range(0, shard_rows, step):
            pick = lax.broadcasted_iota(jnp.int32, (capacity, step), 1) + first == column
            pick = jnp.where(pick, 1.0, 0.0).astype(jnp.bfloat16)
            value = value + jnp.dot(
                pick, table_ref[first : first + step, :], preferred_element_type=jnp.float32
            )
        return value.astype(jnp.bfloat16)

    @pl.loop(1, devices)
    def _(k):
        ask(k).wait_recv()
        found[before(k)] = rows_for(before(k))
        answer(k).start()

    arrived[me] = rows_for(me)

    chunk = pairs // 4

    def gather_in(source):
        rows = arrived[source]
        for first in range(0, pairs, chunk):
            places = place_ref[first : first + chunk, :] - source * capacity
            lane = lax.broadcasted_iota(jnp.int32, (chunk, capacity), 1)
            hit = lane == places[:, 0:1]
            for bag in range(1, bags):
                hit = hit | (lane == places[:, bag : bag + 1])
            hit = jnp.where(hit, 1.0, 0.0).astype(jnp.bfloat16)
            total[first : first + chunk, :] += jnp.dot(hit, rows, preferred_element_type=jnp.float32)

    gather_in(me)

    @pl.loop(1, devices)
    def _(k):
        answer(k).wait_recv()
        gather_in(after(k))

    for feature in range(pairs // samples):
        out_ref[:, feature * row_width : (feature + 1) * row_width] = total[
            feature * samples : (feature + 1) * samples, :
        ].astype(out_ref.dtype)
    asked_ref[...] = asked[...]

    @pl.loop(1, devices)
    def _(k):
        ask(k).wait_send()
        answer(k).wait_send()


def fetch(slots, places, base, table, samples):
    devices, capacity = slots.shape
    pairs, row_width = base.shape
    whole = pl.BlockSpec(memory_space=pltpu.VMEM)
    block = (devices, capacity, row_width)
    first_input, asked = pl.pallas_call(
        functools.partial(fetch_kernel, devices),
        in_specs=[whole] * 4,
        out_specs=[whole] * 2,
        out_shape=[
            jax.ShapeDtypeStruct((samples, pairs // samples * row_width), jnp.bfloat16),
            jax.ShapeDtypeStruct((devices, 1, capacity), jnp.int32),
        ],
        scratch_shapes=[
            pltpu.VMEM((devices, 1, capacity), jnp.int32),
            pltpu.VMEM(block, jnp.bfloat16),
            pltpu.VMEM(block, jnp.bfloat16),
            pltpu.VMEM((pairs, row_width), jnp.float32),
        ]
        + [pltpu.SemaphoreType.DMA((devices,))] * 4,
        compiler_params=pltpu.CompilerParams(
            collective_id=1, has_side_effects=True, vmem_limit_bytes=32 * 1024 * 1024
        ),
    )(slots.reshape(devices, 1, capacity), places, base, table)
    return first_input, asked.reshape(devices, capacity)


def contract_rows(former, latter):
    return lax.dot_general(
        former, latter, (((0,), (0,)), ((), ())), preferred_element_type=jnp.float32
    )


def contract_cols(former, latter):
    return lax.dot_general(
        former, latter, (((1,), (1,)), ((), ())), preferred_element_type=jnp.float32
    )


def per_device(
    ids,
    location,
    cold_table,
    hot_index,
    hot_list,
    hot_table,
    labels,
    cross_u,
    cross_v,
    cross_bias,
    mlp_weight,
    mlp_bias,
    out_weight,
):
    devices = lax.axis_size(BOTH)
    samples, features, bag_size = ids.shape
    shard_rows, row_width = cold_table.shape
    pairs = samples * features
    requests = pairs * bag_size
    mean_load = requests // devices
    capacity = -(-(mean_load + mean_load // 2) // 16) * 16
    placed = look_up(location, ids.transpose(2, 1, 0).reshape(requests))
    owners = placed // shard_rows
    row_slot = placed - owners * shard_rows
    by_owner = owners[:, None] == jnp.arange(devices, dtype=jnp.int32)[None, :]
    member = by_owner.astype(jnp.bfloat16)
    counted = rank_among(member, samples)
    rank = jnp.sum(jnp.where(by_owner, counted, 0.0), axis=1).astype(jnp.int32)
    position = owners * capacity + rank
    ranked = rank[:, None] == jnp.arange(capacity, dtype=jnp.int32)[None, :]
    pair = jnp.arange(requests, dtype=jnp.int32) % pairs
    tables = digits_of(row_slot + 1, shard_rows + 1)
    cut = len(tables)
    tables = tables + digits_of(pair, pairs)
    sheet = jnp.concatenate(
        [jnp.where(ranked, part.astype(jnp.float32)[:, None], 0.0) for part in tables], axis=1
    ).astype(jnp.bfloat16)
    laid = contract_rows(member, sheet).astype(jnp.int32)

    def joined(first, last):
        total = 0
        for place in range(first, last):
            total = total + laid[:, place * capacity : (place + 1) * capacity] * (256 ** (place - first))
        return total

    send_slot = joined(0, cut)
    source = joined(cut, len(tables)).reshape(devices * capacity)
    hot_slots = hot_list.shape[1]
    hot_flat = hot_index.transpose(1, 0).reshape(pairs)
    selector = (hot_flat[:, None] == jnp.arange(hot_slots, dtype=jnp.int32)[None, :]).astype(jnp.bfloat16)
    pooled = jnp.dot(selector, hot_table[hot_list[0]], preferred_element_type=jnp.float32)
    places = position.reshape(bag_size, pairs).transpose(1, 0)
    first_input, wanted = fetch(send_slot, places, pooled, cold_table, samples)
    held = (wanted - 1).reshape(devices, 1, capacity)
    flat = lax.axis_index("grp") * lax.axis_size("dev") + lax.axis_index("dev")
    quad = row_width // hot_slots
    inside = jnp.arange(row_width, dtype=jnp.int32) // hot_slots == flat % quad
    digits = (hot_list[0] // 64, hot_list[0] % 64)
    lists = jnp.stack([jnp.where(inside, jnp.tile(digit, quad), 0) for digit in digits])
    (
        mlp_weight_grad,
        cross_u_grad,
        cross_v_grad,
        mlp_bias_grad,
        out_weight_grad,
        cross_bias_grad,
        hot_grad,
        cold_grad,
    ) = train(
        first_input,
        cross_u,
        cross_v,
        cross_bias[None, :],
        mlp_weight,
        mlp_bias[None, :],
        out_weight.astype(jnp.float32)[None, :],
        labels[None, :],
        source.reshape(devices, 1, capacity),
        held,
        hot_flat[None, :],
        lists.astype(jnp.float32),
        hot_slots,
        hot_table.shape[0],
        shard_rows,
    )
    return (
        cold_grad,
        hot_grad,
        mlp_weight_grad,
        cross_u_grad,
        cross_v_grad,
        cross_bias_grad.reshape(-1),
        mlp_bias_grad.reshape(-1),
        out_weight_grad.reshape(-1),
    )


def solution(mesh):
    placed = (
        P(("grp", "dev"), None, None),
        P(),
        P(("grp", "dev"), None),
        P(("grp", "dev"), None),
        P(("grp", "dev"), None),
        P(),
        P(("grp", "dev")),
        P(),
        P(),
        P(),
        P(),
        P(),
        P(),
    )
    return jax.shard_map(
        per_device,
        mesh=mesh,
        in_specs=placed,
        out_specs=(P(("grp", "dev"), None), P(), P(("grp", "dev"), None), P(), P(), P(), P(), P()),
        check_vma=False,
    )
```

```python
import functools
import math

import jax
import jax.numpy as jnp
from jax import lax
from jax.experimental import pallas as pl
from jax.experimental.pallas import tpu as pltpu
from jax.sharding import PartitionSpec as P

BOTH = ("grp", "dev")


def digits_of(values, limit):
    parts = []
    while limit > 1:
        parts.append(values % 256)
        values = values // 256
        limit = -(-limit // 256)
    return parts


def look_up(table, index):
    size = table.shape[0]
    lanes = 128
    rows = size // lanes
    parts = digits_of(table.reshape(rows, lanes), size)
    stacked = jnp.concatenate(parts, axis=1).astype(jnp.bfloat16)
    pick = (index[:, None] // lanes == jnp.arange(rows, dtype=jnp.int32)[None, :]).astype(jnp.bfloat16)
    found = jnp.dot(pick, stacked, preferred_element_type=jnp.float32)
    lane = (index[:, None] % lanes) == jnp.arange(lanes, dtype=jnp.int32)[None, :]
    total = 0.0
    for place in range(len(parts)):
        total = total + found[:, place * lanes : (place + 1) * lanes] * float(256**place)
    return jnp.sum(jnp.where(lane, total, 0.0), axis=1).astype(jnp.int32)


def rank_among(member, block):
    count, width = member.shape
    pieces = member.reshape(count // block, block, width)
    below = jnp.tril(jnp.ones((block, block), jnp.bfloat16), -1)
    inner = jnp.einsum("ij,bjd->bid", below, pieces, preferred_element_type=jnp.float32)
    sums = jnp.sum(pieces.astype(jnp.float32), axis=1)
    over = jnp.tril(jnp.ones((count // block, count // block), jnp.bfloat16), -1)
    outer = jnp.dot(over, sums.astype(jnp.bfloat16), preferred_element_type=jnp.float32)
    return (inner + outer[:, None, :]).reshape(count, width)


def tiles(width, step=256):
    return [slice(first, min(first + step, width)) for first in range(0, width, step)]


def train_kernel(
    groups,
    stack,
    input_ref,
    cross_u_ref,
    cross_v_ref,
    cross_bias_ref,
    mlp_hbm,
    mlp_bias_ref,
    out_weight_ref,
    label_ref,
    source_ref,
    held_ref,
    hot_ref,
    list_ref,
    mlp_out,
    cross_u_out,
    cross_v_out,
    hidden_bias_out,
    out_weight_out,
    cross_bias_out,
    hot_out,
    cold_out,
    mlp_ref,
    flat_uv,
    term_buf,
    hidden_buf,
    squash_buf,
    active_buf,
    grad_buf,
    turned_buf,
    pool_buf,
    slope_buf,
    pair_buf,
    sums_buf,
    part_mlp,
    part_uv,
    grad_rows,
    outs_all,
    turned_all,
    pair_mlp,
    sum_mlp,
    end_mlp,
    pair_uv,
    sum_uv,
    in_uv,
    zsum_uv,
    end_uv,
    all_uv,
    all_small,
    cold_in,
    send_sem,
    recv_sem,
    row_send,
    row_recv,
    load_sem,
):
    g = lax.axis_index("grp")
    d = lax.axis_index("dev")
    z = lax.div(d, 2)
    c = lax.rem(d, 2)
    half = jnp.bfloat16
    mesh_id = pl.DeviceIdType.MESH
    samples, width = input_ref.shape
    rank = cross_v_ref.shape[0]
    hidden_width = mlp_ref.shape[0]
    rows = mlp_out.shape[0]
    uv_rows = part_uv.shape[3]
    capacity = source_ref.shape[-1]
    pairs, row_width = pair_buf.shape
    hot_slots = all_small.shape[3] - sums_buf.shape[0]
    devices = groups * stack * 2
    me = g * (stack * 2) + d

    def turn(here, by, size):
        return lax.rem(here + by, size)

    def spot(flat):
        return (lax.div(flat, stack * 2), lax.rem(flat, stack * 2))

    def wide(value):
        return value.astype(jnp.float32)

    def dot(former, latter):
        return jnp.dot(former, latter, preferred_element_type=jnp.float32)

    def turned(value):
        return wide(value).T.astype(half)

    started = []

    def send(source, target, to_g, to_z, to_c):
        place = len(started)
        copy = pltpu.make_async_remote_copy(
            src_ref=source,
            dst_ref=target,
            send_sem=send_sem.at[place],
            recv_sem=recv_sem.at[place],
            device_id=(to_g, to_z * 2 + to_c),
            device_id_type=mesh_id,
        )
        copy.start()
        started.append(copy)
        return copy

    def landed(copies):
        for copy in copies:
            copy.wait_recv()

    def own_rows(flat):
        return pl.ds(pl.multiple_of(flat * capacity, 16), capacity)

    def hand(k):
        to = turn(me, k, devices)
        return pltpu.make_async_remote_copy(
            src_ref=grad_rows.at[to],
            dst_ref=cold_in.at[me],
            send_sem=row_send.at[k],
            recv_sem=row_recv.at[k],
            device_id=spot(to),
            device_id_type=mesh_id,
        )

    barrier = pltpu.get_barrier_semaphore()

    @pl.loop(1, devices)
    def _(k):
        pl.semaphore_signal(barrier, inc=1, device_id=spot(turn(me, k, devices)), device_id_type=mesh_id)

    loads = []
    for place, cols in enumerate(tiles(hidden_width)):
        loads.append(pltpu.make_async_copy(mlp_hbm.at[cols], mlp_ref.at[cols], load_sem.at[place]))
        loads[-1].start()

    low = dot(input_ref[...], cross_u_ref[...]).astype(half)
    for cols in tiles(width):
        term = dot(low, cross_v_ref[:, cols]) + cross_bias_ref[cols][None, :]
        value = wide(input_ref[:, cols])
        term_buf[:, cols] = term
        outs_all[g, :, cols] = (value * term + value).astype(half)

    pl.semaphore_wait(barrier, devices - 1)
    paired = groups == 4
    across = lax.div(g, 2) * 2 + 1 - lax.rem(g, 2)
    along = turn(g, 2, groups)
    middle = (width // row_width + 1) // 2 * row_width
    left, right = slice(0, middle), slice(middle, width)

    def send_outs(block, cols, to_g):
        piece = outs_all.at[block, :, cols]
        return send(piece, piece, to_g, z, c)

    if paired:
        outs_first = [send_outs(g, left, across), send_outs(g, right, along)]
        outs_sent = [send_outs(g, right, across), send_outs(g, left, along)]
    else:
        outs_sent = [send_outs(g, slice(0, width), turn(g, k, groups)) for k in range(1, groups)]

    score = jnp.zeros((samples, 1), jnp.float32)
    for load, cols in zip(loads, tiles(hidden_width)):
        load.wait()
        value = contract_cols(outs_all[g], mlp_ref[cols, :]) + mlp_bias_ref[cols][None, :]
        squash = jax.nn.sigmoid(value)
        active = (value * squash).astype(half)
        hidden_buf[:, cols] = value
        squash_buf[:, cols] = squash
        active_buf[:, cols] = active
        score = score + jnp.sum(wide(active) * out_weight_ref[cols][None, :], axis=1, keepdims=True)

    square = (samples, samples)
    diagonal = lax.broadcasted_iota(jnp.int32, square, 0) == lax.broadcasted_iota(jnp.int32, square, 1)
    label = jnp.sum(jnp.where(diagonal, wide(label_ref[...]), 0.0), axis=1, keepdims=True)
    score_grad = jax.nn.sigmoid(score) - label

    sums_buf[...] = jnp.zeros_like(sums_buf)

    def keep_sum(first, cols, value):
        start = first + cols.start // row_width
        for place in range(value.shape[1] // row_width):
            sums_buf[start + place : start + place + 1, :] = value[:, place * row_width : (place + 1) * row_width]

    hidden_rows, width_rows = hidden_width // row_width, width // row_width
    bias_at, out_at, cross_at = 0, hidden_rows, 2 * hidden_rows
    list_at = cross_at + width_rows
    sums_buf[list_at : list_at + 2, :] = list_ref[...]
    share = hidden_width // groups
    for cols in tiles(hidden_width):
        value = hidden_buf[:, cols]
        squash = squash_buf[:, cols]
        slope = squash * (1.0 + value * (1.0 - squash))
        grad = (score_grad * out_weight_ref[cols][None, :] * slope).astype(half)
        grad_buf[:, cols] = grad
        keep_sum(bias_at, cols, jnp.sum(wide(grad), axis=0, keepdims=True))
        keep_sum(out_at, cols, jnp.sum(wide(active_buf[:, cols]) * score_grad, axis=0, keepdims=True))
        inside = cols.start % share
        turned_buf[cols.start // share, inside : inside + cols.stop - cols.start, :] = turned(grad)
    turned_all[g] = turned_buf[g]

    for cols in tiles(width):
        back = dot(grad_buf[...], mlp_ref[:, cols])
        slope = (back * wide(input_ref[:, cols])).astype(half)
        slope_buf[:, cols] = slope
        pool_buf[:, cols] = back * (term_buf[:, cols] + 1.0)
        keep_sum(cross_at, cols, jnp.sum(wide(slope), axis=0, keepdims=True))

    def keep_uv(first, cols, part):
        for place in range(rank // uv_rows):
            flat = first // uv_rows + place
            block, level, core = flat // (stack * 2), flat // 2 % stack, flat % 2
            part_uv[block, level, core, :, cols] = part[place * uv_rows : (place + 1) * uv_rows]

    for flat in range(2 * rank // uv_rows, devices):
        block, level, core = flat // (stack * 2), flat // 2 % stack, flat % 2
        part_uv[block, level, core] = jnp.zeros((uv_rows, width), half)
    low_grad = contract_cols(slope_buf[...], cross_v_ref[...]).astype(half)
    low_turned = turned(low)
    grad_turned = turned(low_grad)
    for cols in tiles(width):
        keep_uv(0, cols, dot(grad_turned, input_ref[:, cols]).astype(half))
        keep_uv(rank, cols, dot(low_turned, slope_buf[:, cols]).astype(half))
    order = [turn(g, k, groups) for k in range(1, groups)] + [g]
    uv_pair = [send(part_uv.at[block, :, 1 - c], pair_uv.at[block], g, z, 1 - c) for block in order]

    for cols in tiles(width):
        value = (pool_buf[:, cols] + contract_cols(low_grad, cross_u_ref[cols, :])).astype(half)
        for place in range(value.shape[1] // row_width):
            feature = cols.start // row_width + place
            pair_buf[feature * samples : (feature + 1) * samples, :] = value[
                :, place * row_width : (place + 1) * row_width
            ]

    spots = (hot_slots, pairs)
    pick = lax.broadcasted_iota(jnp.int32, spots, 0) == hot_ref[...]
    pick = jnp.where(pick, 1.0, 0.0).astype(half)
    all_small[g, z, c, :hot_slots, :] = dot(pick, pair_buf[...]).astype(half)
    all_small[g, z, c, hot_slots:, :] = sums_buf[...].astype(half)
    own = all_small.at[g, z, c]
    small_z = [send(own, own, g, turn(z, k, stack), c) for k in range(1, stack)]

    uv_g = []
    for k, block in enumerate(order):
        landed(uv_pair[k : k + 1])

        @pl.loop(0, stack)
        def _(level, block=block):
            sum_uv[block, level] = (wide(part_uv[block, level, c]) + wide(pair_uv[block, level])).astype(half)

        if k < groups - 1:
            uv_g.append(send(sum_uv.at[block], in_uv.at[k], block, z, c))

    cells = (capacity, capacity)
    corner = lax.broadcasted_iota(jnp.int32, cells, 0) == lax.broadcasted_iota(jnp.int32, cells, 1)

    def rows_for(to):
        wish = source_ref[to].astype(jnp.float32)
        column = jnp.sum(jnp.where(corner, wish, 0.0), axis=1, keepdims=True).astype(jnp.int32)
        pick = lax.broadcasted_iota(jnp.int32, (capacity, pairs), 1) == column
        pick = jnp.where(pick, 1.0, 0.0).astype(half)
        return dot(pick, pair_buf[...]).astype(half)

    def give(first, last):
        @pl.loop(first, last)
        def _(k):
            to = turn(me, k, devices)
            grad_rows[to] = rows_for(to)
            hand(k).start()

    def add_rows_of(source):
        index = held_ref[source]
        grads = cold_in[source]
        step = 256
        for first in range(0, cold_out.shape[0], step):
            pick = lax.broadcasted_iota(jnp.int32, (step, capacity), 0) + first == index
            pick = jnp.where(pick, 1.0, 0.0).astype(half)
            cold_out[first : first + step, :] += dot(pick, grads)

    def take(first, last):
        @pl.loop(first, last)
        def _(k):
            hand(k).wait_recv()
            add_rows_of(turn(me, devices - k, devices))

    def part_of(eighths):
        return max(devices * eighths // 8, 1)

    if paired:
        landed(outs_first)
        outs_sent += [send_outs(across, left, along), send_outs(along, right, across)]
    turned_sent = []
    for k in range(1, groups):
        to_g = turn(g, k, groups)
        turned_sent.append(send(turned_buf.at[to_g], turned_all.at[g], to_g, z, c))
    give(1, part_of(3))

    landed(uv_g)

    @pl.loop(0, stack)
    def _(level):
        value = wide(sum_uv[g, level])
        for k in range(groups - 1):
            value = value + wide(in_uv[k, level])
        zsum_uv[level] = value.astype(half)

    uv_z = []
    for k in range(1, stack):
        to_z = turn(z, k, stack)
        uv_z.append(send(zsum_uv.at[to_z], end_uv.at[k - 1], g, to_z, c))

    give(part_of(3), part_of(5))

    landed(uv_z)
    value = wide(zsum_uv[z])
    for k in range(stack - 1):
        value = value + wide(end_uv[k])
    all_uv[g, z, c] = value.astype(half)
    own = all_uv.at[g, z, c]
    all_z = [send(own, own, g, turn(z, k, stack), c) for k in range(1, stack)]
    landed(outs_sent)
    landed(turned_sent)
    former = jnp.concatenate([turned_all[block] for block in range(groups)], axis=1)
    for cols in tiles(width):
        latter = outs_all[:, :, cols].reshape(groups * samples, cols.stop - cols.start)
        part = dot(former, latter).astype(half)
        for level in range(stack):
            for core in range(2):
                first = (level * 2 + core) * rows
                part_mlp[level, core, :, cols] = part[first : first + rows]
    mlp_pair = [send(part_mlp.at[:, 1 - c], pair_mlp, g, z, 1 - c)]

    give(part_of(5), devices)

    landed(mlp_pair)

    @pl.loop(0, stack)
    def _(level):
        sum_mlp[level] = (wide(part_mlp[level, c]) + wide(pair_mlp[level])).astype(half)

    mlp_z = []

    def send_mlp(first, last):
        for k in range(first, last):
            to_z = turn(z, k, stack)
            mlp_z.append(send(sum_mlp.at[to_z], end_mlp.at[k - 1], g, to_z, c))

    send_mlp(1, stack)
    landed(small_z)
    column = all_small.at[g, :, c]
    small_g = [send(column, column, turn(g, k, groups), z, c) for k in range(1, groups)]
    cold_in[me] = rows_for(me)
    cold_out[...] = jnp.zeros_like(cold_out)
    add_rows_of(me)

    landed(all_z)
    column = all_uv.at[g, :, c]
    all_g = [send(column, column, turn(g, k, groups), z, c) for k in range(1, groups)]
    landed(small_g)
    parity = all_small.at[:, :, c]
    small_c = [send(parity, parity, g, z, 1 - c)]
    take(1, part_of(4))

    landed(all_g)
    parity = all_uv.at[:, :, c]
    all_c = [send(parity, parity, g, z, 1 - c)]
    landed(small_c)

    @pl.loop(0, groups, init_carry=jnp.zeros(sums_buf.shape, jnp.float32))
    def added(block, total):
        for level in range(stack):
            for core in range(2):
                total = total + wide(all_small[block, level, core, hot_slots:, :])
        return total

    hidden_bias_out[...] = added[bias_at:out_at]
    out_weight_out[...] = added[out_at:cross_at]
    cross_bias_out[...] = added[cross_at:list_at]
    hot_out[...] = jnp.zeros_like(hot_out)
    quad = row_width // hot_slots

    def listed(block, level):
        total = jnp.zeros(sums_buf.shape, jnp.float32)
        for place in range(quad):
            total = total + wide(all_small[block, level + place // 2, place % 2, hot_slots:, :])
        row = total[list_at : list_at + 1] * 64.0 + total[list_at + 1 : list_at + 2]
        return row.astype(jnp.int32)

    @pl.loop(0, groups)
    def _(block):
        @pl.loop(0, stack // quad)
        def _(part):
            level = part * quad
            levels = [level, level + quad // 2]
            index = jnp.concatenate([listed(block, first) for first in levels], axis=1)
            grads = all_small[block, pl.ds(level, quad), :, :hot_slots, :]
            grads = grads.reshape(2 * quad * hot_slots, row_width)
            step = 512
            for first in range(0, hot_out.shape[0], step):
                pick = lax.broadcasted_iota(jnp.int32, (step, 2 * row_width), 0) + first == index
                pick = jnp.where(pick, 1.0, 0.0).astype(half)
                hot_out[first : first + step, :] += dot(pick, grads)

    take(part_of(4), devices)

    landed(mlp_z)
    value = wide(sum_mlp[z])
    for k in range(stack - 1):
        value = value + wide(end_mlp[k])
    mlp_out[...] = value

    landed(all_c)
    for flat in range(2 * rank // uv_rows):
        block, level, core = flat // (stack * 2), flat // 2 % stack, flat % 2
        first = flat * uv_rows
        if first < rank:
            flat_uv[first : first + uv_rows, :] = wide(all_uv[block, level, core])
        else:
            cross_v_out[first - rank : first - rank + uv_rows, :] = wide(all_uv[block, level, core])
    for cols in tiles(width):
        cross_u_out[cols, :] = flat_uv[:, cols].T

    for copy in started:
        copy.wait_send()

    @pl.loop(1, devices)
    def _(k):
        hand(k).wait_send()


def train(first_input, cross_u, cross_v, cross_bias, mlp_weight, mlp_bias, out_weight, labels, source, held, hot, lists, hot_slots, hot_rows, shard_rows):
    groups = lax.axis_size("grp")
    stack = lax.axis_size("dev") // 2
    devices = groups * stack * 2
    samples, width = first_input.shape
    rank = cross_v.shape[0]
    hidden_width = mlp_weight.shape[0]
    rows = hidden_width // devices
    uv_rows = -(-2 * rank // (16 * devices)) * 16
    capacity = source.shape[-1]
    row_width = lists.shape[1]
    pairs = hot.shape[1]
    half, full = jnp.bfloat16, jnp.float32
    sum_rows = 2 + (width + 2 * hidden_width) // row_width
    sum_rows = -(-sum_rows // 16) * 16
    small_rows = hot_slots + sum_rows
    share = hidden_width // groups
    lead = (groups, stack, 2)
    scratch = [
        ((hidden_width, width), half),
        ((rank, width), full),
        ((samples, width), full),
        ((samples, hidden_width), full),
        ((samples, hidden_width), full),
        ((samples, hidden_width), half),
        ((samples, hidden_width), half),
        ((groups, share, samples), half),
        ((samples, width), full),
        ((samples, width), half),
        ((pairs, row_width), half),
        ((sum_rows, row_width), full),
        ((stack, 2, rows, width), half),
        (lead + (uv_rows, width), half),
        ((devices, capacity, row_width), half),
        ((groups, samples, width), half),
        ((groups, share, samples), half),
        ((stack, rows, width), half),
        ((stack, rows, width), half),
        ((stack - 1, rows, width), half),
        ((groups, stack, uv_rows, width), half),
        ((groups, stack, uv_rows, width), half),
        ((groups - 1, stack, uv_rows, width), half),
        ((stack, uv_rows, width), half),
        ((stack - 1, uv_rows, width), half),
        (lead + (uv_rows, width), half),
        (lead + (small_rows, row_width), half),
        ((devices, capacity, row_width), half),
    ]
    outs = [
        ((rows, width), full),
        ((width, rank), full),
        ((rank, width), full),
        ((hidden_width // row_width, row_width), full),
        ((hidden_width // row_width, row_width), full),
        ((width // row_width, row_width), full),
        ((hot_rows, row_width), full),
        ((shard_rows, row_width), full),
    ]
    copies = 5 * (groups - 1) + 3 + groups + 4 * (stack - 1) + 3
    whole = pl.BlockSpec(memory_space=pltpu.VMEM)
    args = (first_input, cross_u, cross_v, cross_bias, mlp_weight, mlp_bias, out_weight, labels, source, held, hot, lists)
    size = sum(math.prod(shape) * jnp.dtype(kind).itemsize for shape, kind in scratch + outs)
    size += sum(arg.size * arg.dtype.itemsize for arg in args) - mlp_weight.size * 2 + devices * capacity * 64
    limit = min(size + 6 * 1024 * 1024, 61 * 1024 * 1024)
    return pl.pallas_call(
        functools.partial(train_kernel, groups, stack),
        in_specs=[whole] * 4 + [pl.BlockSpec(memory_space=pl.ANY)] + [whole] * (len(args) - 5),
        out_specs=[whole] * len(outs),
        out_shape=[jax.ShapeDtypeStruct(shape, kind) for shape, kind in outs],
        scratch_shapes=[pltpu.VMEM(shape, kind) for shape, kind in scratch]
        + [pltpu.SemaphoreType.DMA((copies,))] * 2
        + [pltpu.SemaphoreType.DMA((devices,))] * 2
        + [pltpu.SemaphoreType.DMA((len(tiles(hidden_width)),))],
        compiler_params=pltpu.CompilerParams(collective_id=0, has_side_effects=True, vmem_limit_bytes=limit),
    )(*args)


def fetch_kernel(
    devices,
    slot_ref,
    place_ref,
    base_ref,
    table_ref,
    out_ref,
    asked_ref,
    asked,
    found,
    arrived,
    total,
    ask_send,
    ask_recv,
    row_send,
    row_recv,
):
    per_group = lax.axis_size("dev")
    me = lax.axis_index("grp") * per_group + lax.axis_index("dev")
    mesh_id = pl.DeviceIdType.MESH
    capacity = slot_ref.shape[-1]
    shard_rows, row_width = table_ref.shape
    pairs, bags = place_ref.shape
    samples = out_ref.shape[0]

    def spot(flat):
        return (lax.div(flat, per_group), lax.rem(flat, per_group))

    def after(k):
        return lax.rem(me + k, devices)

    def before(k):
        return lax.rem(me + devices - k, devices)

    def ask(k):
        return pltpu.make_async_remote_copy(
            src_ref=slot_ref.at[after(k)],
            dst_ref=asked.at[me],
            send_sem=ask_send.at[k],
            recv_sem=ask_recv.at[k],
            device_id=spot(after(k)),
            device_id_type=mesh_id,
        )

    def answer(k):
        return pltpu.make_async_remote_copy(
            src_ref=found.at[before(k)],
            dst_ref=arrived.at[me],
            send_sem=row_send.at[k],
            recv_sem=row_recv.at[k],
            device_id=spot(before(k)),
            device_id_type=mesh_id,
        )

    barrier = pltpu.get_barrier_semaphore()

    @pl.loop(1, devices)
    def _(k):
        pl.semaphore_signal(barrier, inc=1, device_id=spot(after(k)), device_id_type=mesh_id)

    pl.semaphore_wait(barrier, devices - 1)

    @pl.loop(1, devices)
    def _(k):
        ask(k).start()

    asked[me] = slot_ref[me]
    total[...] = base_ref[...]

    square = (capacity, capacity)
    diagonal = lax.broadcasted_iota(jnp.int32, square, 0) == lax.broadcasted_iota(jnp.int32, square, 1)

    def rows_for(owner_of):
        wish = asked[owner_of].astype(jnp.float32)
        column = jnp.sum(jnp.where(diagonal, wish, 0.0), axis=1, keepdims=True).astype(jnp.int32) - 1
        value = jnp.zeros((capacity, row_width), jnp.float32)
        step = 512
        for first in range(0, shard_rows, step):
            pick = lax.broadcasted_iota(jnp.int32, (capacity, step), 1) + first == column
            pick = jnp.where(pick, 1.0, 0.0).astype(jnp.bfloat16)
            value = value + jnp.dot(
                pick, table_ref[first : first + step, :], preferred_element_type=jnp.float32
            )
        return value.astype(jnp.bfloat16)

    @pl.loop(1, devices)
    def _(k):
        ask(k).wait_recv()
        found[before(k)] = rows_for(before(k))
        answer(k).start()

    arrived[me] = rows_for(me)

    chunk = pairs // 4

    def gather_in(source):
        rows = arrived[source]
        for first in range(0, pairs, chunk):
            places = place_ref[first : first + chunk, :] - source * capacity
            lane = lax.broadcasted_iota(jnp.int32, (chunk, capacity), 1)
            hit = lane == places[:, 0:1]
            for bag in range(1, bags):
                hit = hit | (lane == places[:, bag : bag + 1])
            hit = jnp.where(hit, 1.0, 0.0).astype(jnp.bfloat16)
            total[first : first + chunk, :] += jnp.dot(hit, rows, preferred_element_type=jnp.float32)

    gather_in(me)

    @pl.loop(1, devices)
    def _(k):
        answer(k).wait_recv()
        gather_in(after(k))

    for feature in range(pairs // samples):
        out_ref[:, feature * row_width : (feature + 1) * row_width] = total[
            feature * samples : (feature + 1) * samples, :
        ].astype(out_ref.dtype)
    asked_ref[...] = asked[...]

    @pl.loop(1, devices)
    def _(k):
        ask(k).wait_send()
        answer(k).wait_send()


def fetch(slots, places, base, table, samples):
    devices, capacity = slots.shape
    pairs, row_width = base.shape
    whole = pl.BlockSpec(memory_space=pltpu.VMEM)
    block = (devices, capacity, row_width)
    first_input, asked = pl.pallas_call(
        functools.partial(fetch_kernel, devices),
        in_specs=[whole] * 4,
        out_specs=[whole] * 2,
        out_shape=[
            jax.ShapeDtypeStruct((samples, pairs // samples * row_width), jnp.bfloat16),
            jax.ShapeDtypeStruct((devices, 1, capacity), jnp.int32),
        ],
        scratch_shapes=[
            pltpu.VMEM((devices, 1, capacity), jnp.int32),
            pltpu.VMEM(block, jnp.bfloat16),
            pltpu.VMEM(block, jnp.bfloat16),
            pltpu.VMEM((pairs, row_width), jnp.float32),
        ]
        + [pltpu.SemaphoreType.DMA((devices,))] * 4,
        compiler_params=pltpu.CompilerParams(
            collective_id=1, has_side_effects=True, vmem_limit_bytes=32 * 1024 * 1024
        ),
    )(slots.reshape(devices, 1, capacity), places, base, table)
    return first_input, asked.reshape(devices, capacity)


def contract_rows(former, latter):
    return lax.dot_general(
        former, latter, (((0,), (0,)), ((), ())), preferred_element_type=jnp.float32
    )


def contract_cols(former, latter):
    return lax.dot_general(
        former, latter, (((1,), (1,)), ((), ())), preferred_element_type=jnp.float32
    )


def per_device(
    ids,
    location,
    cold_table,
    hot_index,
    hot_list,
    hot_table,
    labels,
    cross_u,
    cross_v,
    cross_bias,
    mlp_weight,
    mlp_bias,
    out_weight,
):
    devices = lax.axis_size(BOTH)
    samples, features, bag_size = ids.shape
    shard_rows, row_width = cold_table.shape
    pairs = samples * features
    requests = pairs * bag_size
    mean_load = requests // devices
    capacity = -(-(mean_load + mean_load // 2) // 16) * 16
    placed = look_up(location, ids.transpose(2, 1, 0).reshape(requests))
    owners = placed // shard_rows
    row_slot = placed - owners * shard_rows
    by_owner = owners[:, None] == jnp.arange(devices, dtype=jnp.int32)[None, :]
    member = by_owner.astype(jnp.bfloat16)
    counted = rank_among(member, samples)
    rank = jnp.sum(jnp.where(by_owner, counted, 0.0), axis=1).astype(jnp.int32)
    position = owners * capacity + rank
    ranked = rank[:, None] == jnp.arange(capacity, dtype=jnp.int32)[None, :]
    pair = jnp.arange(requests, dtype=jnp.int32) % pairs
    tables = digits_of(row_slot + 1, shard_rows + 1)
    cut = len(tables)
    tables = tables + digits_of(pair, pairs)
    sheet = jnp.concatenate(
        [jnp.where(ranked, part.astype(jnp.float32)[:, None], 0.0) for part in tables], axis=1
    ).astype(jnp.bfloat16)
    laid = contract_rows(member, sheet).astype(jnp.int32)

    def joined(first, last):
        total = 0
        for place in range(first, last):
            total = total + laid[:, place * capacity : (place + 1) * capacity] * (256 ** (place - first))
        return total

    send_slot = joined(0, cut)
    source = joined(cut, len(tables)).reshape(devices * capacity)
    hot_slots = hot_list.shape[1]
    hot_flat = hot_index.transpose(1, 0).reshape(pairs)
    selector = (hot_flat[:, None] == jnp.arange(hot_slots, dtype=jnp.int32)[None, :]).astype(jnp.bfloat16)
    pooled = jnp.dot(selector, hot_table[hot_list[0]], preferred_element_type=jnp.float32)
    places = position.reshape(bag_size, pairs).transpose(1, 0)
    first_input, wanted = fetch(send_slot, places, pooled, cold_table, samples)
    held = (wanted - 1).reshape(devices, 1, capacity)
    flat = lax.axis_index("grp") * lax.axis_size("dev") + lax.axis_index("dev")
    quad = row_width // hot_slots
    inside = jnp.arange(row_width, dtype=jnp.int32) // hot_slots == flat % quad
    digits = (hot_list[0] // 64, hot_list[0] % 64)
    lists = jnp.stack([jnp.where(inside, jnp.tile(digit, quad), 0) for digit in digits])
    (
        mlp_weight_grad,
        cross_u_grad,
        cross_v_grad,
        mlp_bias_grad,
        out_weight_grad,
        cross_bias_grad,
        hot_grad,
        cold_grad,
    ) = train(
        first_input,
        cross_u,
        cross_v,
        cross_bias,
        mlp_weight,
        mlp_bias,
        out_weight.astype(jnp.float32),
        labels[None, :],
        source.reshape(devices, 1, capacity),
        held,
        hot_flat[None, :],
        lists.astype(jnp.float32),
        hot_slots,
        hot_table.shape[0],
        shard_rows,
    )
    return (
        cold_grad,
        hot_grad,
        mlp_weight_grad,
        cross_u_grad,
        cross_v_grad,
        cross_bias_grad.reshape(-1),
        mlp_bias_grad.reshape(-1),
        out_weight_grad.reshape(-1),
    )


def solution(mesh):
    placed = (
        P(("grp", "dev"), None, None),
        P(),
        P(("grp", "dev"), None),
        P(("grp", "dev"), None),
        P(("grp", "dev"), None),
        P(),
        P(("grp", "dev")),
        P(),
        P(),
        P(),
        P(),
        P(),
        P(),
    )
    return jax.shard_map(
        per_device,
        mesh=mesh,
        in_specs=placed,
        out_specs=(P(("grp", "dev"), None), P(), P(("grp", "dev"), None), P(), P(), P(), P(), P()),
        check_vma=False,
    )
```
